32 devices in a mesh: fsdp: 4 (over y, core), ctx: 8 (over z, x).
Axes of the slice: x: 2, y: 2, z: 4, core: 2. Of those that a mesh axis runs over, the one named last changes fastest.
Arguments:
- query_proj: bfloat16 [4, 1024, 4096], P('fsdp', 'ctx'), may hold values from -10 to 10
- key_proj: bfloat16 [4, 1024, 4096], P('fsdp', 'ctx'), may hold values from -10 to 10
- value_proj: bfloat16 [4, 1024, 4096], P('fsdp', 'ctx'), may hold values from -12 to 12
- modality: int32 [4, 1024], P('fsdp', 'ctx'), may hold values from 0 to 1, as said below
- out_weight: bfloat16 [2, 4096, 2048], P(None, ('fsdp', 'ctx')), may hold values from -0.09375 to 0.09375
- grad_projected: bfloat16 [4, 1024, 2048], P('fsdp', 'ctx'), may hold values from -6 to 6
Outputs:
- projected: bfloat16 [4, 1024, 2048], P('fsdp', 'ctx')
- grad_query: bfloat16 [4, 1024, 4096], P('fsdp', 'ctx')
- grad_key: bfloat16 [4, 1024, 4096], P('fsdp', 'ctx')
- grad_value: bfloat16 [4, 1024, 4096], P('fsdp', 'ctx')
The draws below stay inside these ranges and needn't reach their ends.
Inputs may be any that keep to these rules, and one draw needn't show every extreme that they name: `modality`: each sequence holds exactly two image spans of 256 positions each, one starting within the first half and lying in the first half, the other lying in the second half; all other positions are text, so exactly half of each sequence's positions are image.
All inputs are finite; a program needn't handle non-finite values.
Results may differ from the reference program's by a relative error of at most 0.012.
The reference program's roundings to bfloat16 on the way count: a program that leaves them out, or rounds other values in their place, can miss the bound.
Values may be sent and summed in bfloat16 or wider, within the bound.
A program may use at most 320 MiB of HBM per device.

```python
import jax
import jax.numpy as jnp
from jax import lax

HEAD_COUNT = 32
HEAD_SIZE = 128
OUT_WIDTH = 2048
LENGTH = 1024
IMAGE_SPAN = 256
SEQUENCES = 4


def base_draw(key, offset_tag):
    folded = jax.random.fold_in(key, offset_tag)
    extent = (SEQUENCES, LENGTH, HEAD_COUNT * HEAD_SIZE)
    return jnp.clip(1.3 * jax.random.normal(folded, extent, jnp.float32), -6.0, 6.0)


def draw_query_proj(key, part):
    values = base_draw(key, 11)
    return values.astype(jnp.bfloat16)


def draw_key_proj(key, part):
    values = base_draw(key, 23)
    return values.astype(jnp.bfloat16)


def draw_modality(key, part):
    folded = jax.random.fold_in(key, 5)
    first_key, second_key = jax.random.split(folded, 2)
    first_start = jax.random.randint(first_key, (SEQUENCES,), 0, LENGTH // 2 - IMAGE_SPAN + 1)
    second_start = jax.random.randint(second_key, (SEQUENCES,), LENGTH // 2, LENGTH - IMAGE_SPAN + 1)
    places = jnp.arange(LENGTH)[None, :]
    inside_first = (places >= first_start[:, None]) & (places < first_start[:, None] + IMAGE_SPAN)
    inside_second = (places >= second_start[:, None]) & (places < second_start[:, None] + IMAGE_SPAN)
    return (inside_first | inside_second).astype(jnp.int32)


def block_scale(stream_key, shape, cuts, smallest, top_value):
    gain = 1.0
    for position, blocks in cuts:
        heights = jax.random.uniform(jax.random.fold_in(jax.random.fold_in(stream_key, 6), position), (blocks,), jnp.float32, smallest / len(cuts), top_value / len(cuts))
        gain = gain * jnp.repeat(jnp.exp(heights), shape[position] // blocks).reshape((-1,) + (1,) * (len(shape) - 1 - position))
    return gain


def centred(key, dims, width, reach, cuts=(), kind=jnp.bfloat16):
    values = width * jax.random.normal(key, dims, jnp.float32)
    if cuts:
        values = values * block_scale(key, dims, cuts, -0.22, 0.18)
    return jnp.clip(values, -reach, reach).astype(kind)


def setup_inputs(seed: int = 0) -> dict:
    key_of = jax.random.split(jax.random.key(seed), 7)
    return {
        "query_proj": draw_query_proj(jax.random.fold_in(key_of[6], 71), 0),
        "key_proj": draw_key_proj(jax.random.fold_in(key_of[6], 71), 0),
        "value_proj": centred(key_of[2], (SEQUENCES, LENGTH, HEAD_COUNT * HEAD_SIZE), 2.0, 12.0, ((0, 4), (1, 8))),
        "modality": draw_modality(jax.random.fold_in(key_of[6], 71), 0),
        "out_weight": centred(key_of[4], (2, HEAD_COUNT * HEAD_SIZE, OUT_WIDTH), (HEAD_COUNT * HEAD_SIZE) ** -0.5, 0.09375, ((1, 32),)),
        "grad_projected": centred(key_of[5], (SEQUENCES, LENGTH, OUT_WIDTH), 1.0, 6.0, ((0, 4), (1, 8))),
    }


def block_count(length):
    return max(1, min(8, length // 512))


def rounded(matrix):
    return lax.optimization_barrier(matrix.astype(jnp.bfloat16)).astype(jnp.float32)


def probabilities(query_block, key_prefix, offset):
    scaling = query_block.shape[-1] ** -0.5
    scores = jnp.einsum("qhd,khd->hqk", query_block.astype(jnp.float32), key_prefix.astype(jnp.float32)) * scaling
    query_places = offset + jnp.arange(query_block.shape[0])
    key_places = jnp.arange(key_prefix.shape[0])
    scores = jnp.where(key_places[None, None, :] <= query_places[None, :, None], scores, -jnp.inf)
    highest = jnp.max(scores, axis=-1, keepdims=True)
    raised = jnp.exp(scores - highest)
    return raised / jnp.sum(raised, axis=-1, keepdims=True)


def attend_forward(queries, keys_all, values_all):
    length = queries.shape[0]
    block_rows = length // block_count(length)
    pieces = []
    for block_index in range(length // block_rows):
        offset = block_index * block_rows
        finish = offset + block_rows
        weights = probabilities(queries[offset:finish], keys_all[:finish], offset)
        output = jnp.einsum("hqk,khd->qhd", rounded(weights), values_all[:finish].astype(jnp.float32))
        pieces.append(output.astype(jnp.bfloat16))
    return jnp.concatenate(pieces, axis=0)


def attend_backward(queries, keys_all, values_all, attention, grad_attention):
    length = queries.shape[0]
    block_rows = length // block_count(length)
    scaling = queries.shape[-1] ** -0.5
    grad_keys = jnp.zeros(queries.shape, jnp.float32)
    grad_values = jnp.zeros(queries.shape, jnp.float32)
    query_pieces = []
    for block_index in range(length // block_rows):
        offset = block_index * block_rows
        finish = offset + block_rows
        query_block = queries[offset:finish]
        weights = probabilities(query_block, keys_all[:finish], offset)
        grad_block = grad_attention[offset:finish].astype(jnp.float32)
        attn_block = attention[offset:finish].astype(jnp.float32)
        grad_values = grad_values.at[:finish].add(jnp.einsum("hqk,qhd->khd", rounded(weights), grad_block))
        grad_weights = jnp.einsum("qhd,khd->hqk", grad_block, values_all[:finish].astype(jnp.float32))
        row_delta = jnp.sum(grad_block * attn_block, axis=-1).T[:, :, None]
        grad_scores = rounded(weights * (grad_weights - row_delta) * scaling)
        query_pieces.append(jnp.einsum("hqk,khd->qhd", grad_scores, keys_all[:finish].astype(jnp.float32)).astype(jnp.bfloat16))
        grad_keys = grad_keys.at[:finish].add(jnp.einsum("hqk,qhd->khd", grad_scores, query_block.astype(jnp.float32)))
    return jnp.concatenate(query_pieces, axis=0), grad_keys.astype(jnp.bfloat16), grad_values.astype(jnp.bfloat16)


def reference(query_proj, key_proj, value_proj, modality, out_weight, grad_projected):
    def per_sequence(inputs):
        queries, keys_all, values_all, modal_ids, upstream = inputs
        shaped = (LENGTH, HEAD_COUNT, HEAD_SIZE)
        inner_width = HEAD_COUNT * HEAD_SIZE
        queries = queries.reshape(shaped)
        keys_all = keys_all.reshape(shaped)
        values_all = values_all.reshape(shaped)
        attention = attend_forward(queries, keys_all, values_all)
        flat = attention.reshape(LENGTH, inner_width)
        is_image = (modal_ids == 1)[:, None]
        text_out = jnp.dot(flat, out_weight[0], preferred_element_type=jnp.float32)
        image_out = jnp.dot(flat, out_weight[1], preferred_element_type=jnp.float32)
        result = jnp.where(is_image, image_out, text_out).astype(jnp.bfloat16)
        text_back = jnp.dot(upstream, out_weight[0].T, preferred_element_type=jnp.float32)
        image_back = jnp.dot(upstream, out_weight[1].T, preferred_element_type=jnp.float32)
        grad_attention = jnp.where(is_image, image_back, text_back).astype(jnp.bfloat16).reshape(shaped)
        grad_q, grad_k, grad_v = attend_backward(queries, keys_all, values_all, attention, grad_attention)
        return result, grad_q.reshape(LENGTH, inner_width), grad_k.reshape(LENGTH, inner_width), grad_v.reshape(LENGTH, inner_width)

    projected, grad_query, grad_key, grad_value = lax.map(per_sequence, (query_proj, key_proj, value_proj, modality, grad_projected))
    return (projected, grad_query, grad_key, grad_value)
```

```python
import functools

import jax
import jax.numpy as jnp
from jax import lax
from jax.experimental import pallas as pl
from jax.experimental.pallas import tpu as pltpu
from jax.sharding import PartitionSpec as P

HEAD_SIZE = 128


def block_count(length):
    return max(1, min(8, length // 512))


def probabilities(query_block, key_prefix, offset):
    scaling = query_block.shape[-1] ** (-0.5)
    scores = (
        jnp.einsum("hqd,hkd->hqk", query_block, key_prefix, preferred_element_type=jnp.float32)
        * scaling
    )
    query_places = offset + jnp.arange(query_block.shape[1])
    key_places = jnp.arange(key_prefix.shape[1])
    scores = jnp.where(key_places[None, None, :] <= query_places[None, :, None], scores, -jnp.inf)
    highest = jnp.max(scores, axis=-1, keepdims=True)
    raised = jnp.exp(scores - highest)
    return raised / jnp.sum(raised, axis=-1, keepdims=True)


def attend_forward(queries, keys_all, values_all):
    length = queries.shape[1]
    block_rows = length // block_count(length)
    pieces = []
    for block_index in range(length // block_rows):
        offset = block_index * block_rows
        finish = offset + block_rows
        weights = probabilities(queries[:, offset:finish], keys_all[:, :finish], offset).astype(
            jnp.bfloat16
        )
        output = jnp.einsum(
            "hqk,hkd->hqd", weights, values_all[:, :finish], preferred_element_type=jnp.float32
        )
        pieces.append(output.astype(jnp.bfloat16))
    return jnp.concatenate(pieces, axis=1)


def attend_backward(queries, keys_all, values_all, attention, grad_attention):
    length = queries.shape[1]
    block_rows = length // block_count(length)
    scaling = queries.shape[-1] ** (-0.5)
    grad_keys = jnp.zeros(queries.shape, jnp.float32)
    grad_values = jnp.zeros(queries.shape, jnp.float32)
    query_pieces = []
    for block_index in range(length // block_rows):
        offset = block_index * block_rows
        finish = offset + block_rows
        query_block = queries[:, offset:finish]
        weights = probabilities(query_block, keys_all[:, :finish], offset)
        grad_block = grad_attention[:, offset:finish]
        attn_block = attention[:, offset:finish]
        grad_values = grad_values.at[:, :finish].add(
            jnp.einsum(
                "hqk,hqd->hkd",
                weights.astype(jnp.bfloat16),
                grad_block,
                preferred_element_type=jnp.float32,
            )
        )
        grad_weights = jnp.einsum(
            "hqd,hkd->hqk", grad_block, values_all[:, :finish], preferred_element_type=jnp.float32
        )
        row_delta = jnp.sum(
            grad_block.astype(jnp.float32) * attn_block.astype(jnp.float32), axis=-1, keepdims=True
        )
        grad_scores = (weights * (grad_weights - row_delta) * scaling).astype(jnp.bfloat16)
        query_pieces.append(
            jnp.einsum(
                "hqk,hkd->hqd",
                grad_scores,
                keys_all[:, :finish],
                preferred_element_type=jnp.float32,
            ).astype(jnp.bfloat16)
        )
        grad_keys = grad_keys.at[:, :finish].add(
            jnp.einsum("hqk,hqd->hkd", grad_scores, query_block, preferred_element_type=jnp.float32)
        )
    return (
        jnp.concatenate(query_pieces, axis=1),
        grad_keys.astype(jnp.bfloat16),
        grad_values.astype(jnp.bfloat16),
    )


def transposed_product(left, right):
    return lax.dot_general(
        left, right, (((1,), (1,)), ((), ())), preferred_element_type=jnp.float32
    )


def heads_first(flat, length, local_heads):
    return flat.reshape(length, local_heads, HEAD_SIZE).transpose(1, 0, 2)


def heads_last(stacked, length, local_width):
    return stacked.transpose(1, 0, 2).reshape(1, length, local_width)


def per_device_gathered(query_proj, key_proj, value_proj, modality, out_weight, grad_projected):
    context_size = lax.axis_size("ctx")
    row_count = query_proj.shape[1]
    inner_width = query_proj.shape[2]
    length = row_count * context_size
    local_width = inner_width // context_size
    local_heads = local_width // HEAD_SIZE
    head_query, head_key, head_value = (
        lax.all_to_all(query_proj, "ctx", split_axis=2, concat_axis=1, tiled=True),
        lax.all_to_all(key_proj, "ctx", split_axis=2, concat_axis=1, tiled=True),
        lax.all_to_all(value_proj, "ctx", split_axis=2, concat_axis=1, tiled=True),
    )
    head_query = heads_first(head_query, length, local_heads)
    head_key = heads_first(head_key, length, local_heads)
    head_value = heads_first(head_value, length, local_heads)
    attention = attend_forward(head_query, head_key, head_value)
    sending = heads_last(attention, length, local_width)
    attn_rows = lax.all_to_all(sending, "ctx", split_axis=1, concat_axis=2, tiled=True)[0]
    upstream = grad_projected[0]
    weight_piece = lax.all_gather(out_weight, ("fsdp", "ctx"), axis=1, tiled=True)
    text_out = jnp.dot(attn_rows, weight_piece[0], preferred_element_type=jnp.float32)
    image_out = jnp.dot(attn_rows, weight_piece[1], preferred_element_type=jnp.float32)
    text_grad = transposed_product(upstream, weight_piece[0])
    image_grad = transposed_product(upstream, weight_piece[1])
    text_out, image_out, text_grad, image_grad = (text_out, image_out, text_grad, image_grad)
    image_rows = (modality[0] == 1)[:, None]
    projected = jnp.where(image_rows, image_out, text_out).astype(jnp.bfloat16)[None]
    grad_rows = jnp.where(image_rows, image_grad, text_grad).astype(jnp.bfloat16)
    grad_heads = lax.all_to_all(grad_rows[None], "ctx", split_axis=2, concat_axis=1, tiled=True)
    grad_heads = heads_first(grad_heads, length, local_heads)
    grad_q, grad_k, grad_v = attend_backward(
        head_query, head_key, head_value, attention, grad_heads
    )
    grad_query, grad_key, grad_value = (
        lax.all_to_all(
            heads_last(grad_q, length, local_width), "ctx", split_axis=1, concat_axis=2, tiled=True
        ),
        lax.all_to_all(
            heads_last(grad_k, length, local_width), "ctx", split_axis=1, concat_axis=2, tiled=True
        ),
        lax.all_to_all(
            heads_last(grad_v, length, local_width), "ctx", split_axis=1, concat_axis=2, tiled=True
        ),
    )
    return (projected, grad_query, grad_key, grad_value)


NT = (((1,), (1,)), ((), ()))
TN = (((0,), (0,)), ((), ()))
AHEAD = 4


def middle_kernel(
    groups,
    size,
    q_in, k_in, v_in, w_in, up_in, mark_in,
    proj_out, dq_out, dk_out, dv_out,
    wbuf, kvbuf, qbuf, up, marks, total, gbuf, obuf, dq_buf, dkv_buf, dk_sum, dv_sum,
    part_out, part_in, proj_buf,
    kv_sem, q_sem, lower_sem, rect_sem, w_sem,
    in_send, lower_send, rect_send, dq_send, dkv_send, w_send,
    single, out_sem, part_send, part_sem,
):
    rows = q_in.shape[0]
    levels = size // 2
    steps = groups * levels
    blocks = size // 2
    half = blocks * rows
    scaling = HEAD_SIZE ** (-0.5)
    group, ctx = lax.axis_index("fsdp"), lax.axis_index("ctx")
    place, side = ctx // 2, ctx % 2
    owner_place = levels // 2 - 1 + place // (levels // 2)
    across = (group + 2) % groups
    partner = group + 1 - 2 * (group % 2)
    position = ctx % blocks

    def columns(step, p):
        turn, which = step // groups, step % groups
        source = (2 - turn) + levels * (turn // 3)
        owner = ((group // 2 + which // 2) % 2) * 2 + (group % 2 + which % 2) % 2
        head = owner * size + 2 * source + p
        return pl.ds(pl.multiple_of(head * HEAD_SIZE, HEAD_SIZE), HEAD_SIZE)

    def remote(source, target, send_sem, receive_sem, device):
        return pltpu.make_async_remote_copy(
            src_ref=source,
            dst_ref=target,
            send_sem=send_sem,
            recv_sem=receive_sem,
            device_id=device,
            device_id_type=pl.DeviceIdType.MESH,
        )

    def arrived(ref, sem):
        remote(ref, ref, sem, sem, {"ctx": (ctx + 1) % size}).wait_recv()

    def sent(ref, sem):
        remote(ref, ref, sem, sem, {"ctx": (ctx + 1) % size}).wait_send()

    def deliver(source, target, send_sem, receive_sem, to):
        @pl.when(to == ctx)
        def _():
            pltpu.make_async_copy(source, target, receive_sem).start()

        @pl.when(to != ctx)
        def _():
            remote(source, target, send_sem, receive_sem, {"ctx": to}).start()

    barrier = pltpu.get_barrier_semaphore()
    greeted = [{"ctx": lax.rem(ctx + step, size)} for step in range(1, size)]
    greeted += [{"fsdp": across}, {"fsdp": partner}]
    for peer in greeted:
        pl.semaphore_signal(barrier, 1, device_id=peer, device_id_type=pl.DeviceIdType.MESH)
    pl.semaphore_wait(barrier, len(greeted))

    own_rows = pl.ds(pl.multiple_of(position * rows, rows), rows)
    key_rows = pl.ds(pl.multiple_of(ctx * rows, rows), rows)

    def send_upstream():
        for p in range(2):
            to = owner_place * 2 + p
            deliver(up_in, up.at[own_rows], single.at[0], single.at[1], to)
            deliver(mark_in, marks.at[own_rows], single.at[2], single.at[3], to)

    def send_step(step):
        for p in range(2):
            to, cols = owner_place * 2 + p, columns(step, p)
            deliver(k_in.at[:, cols], kvbuf.at[step, 0, key_rows], in_send.at[step], kv_sem.at[step], to)
            deliver(v_in.at[:, cols], kvbuf.at[step, 1, key_rows], in_send.at[step], kv_sem.at[step], to)
            deliver(q_in.at[:, cols], qbuf.at[step, own_rows], in_send.at[step], q_sem.at[step], to)

    def leaf(lower):
        turn, moment = (2, 2) if lower else (3, 2)
        send_upstream()

        @pl.loop(0, steps)
        def _(step):
            @pl.when(step == moment)
            def _():
                slot = turn * groups
                remote(
                    w_in, wbuf.at[slot], w_send.at[0, 0], w_sem.at[slot],
                    {"ctx": owner_place * 2 + side},
                ).start()

            send_step(step)

        sent(w_in, w_send.at[0, 0])
        sent(up.at[pl.ds(0, 2 * rows)], single.at[0])
        sent(marks.at[pl.ds(0, 2 * rows)], single.at[2])

        @pl.loop(0, steps)
        def _(step):
            sent(kvbuf.at[step, :, pl.ds(0, 3 * rows)], in_send.at[step])

    def compute(step, base):
        both = lax.dot_general(up[...], wbuf[step], NT, preferred_element_type=jnp.float32)
        image = marks[...] > 0.5
        gbuf[...] = jnp.where(image, both[:, HEAD_SIZE:], both[:, :HEAD_SIZE]).astype(jnp.bfloat16)
        span = half // 2
        for block in reversed(range(2)):
            offset = block * span
            finish = base + offset + span
            q = qbuf[step, offset : offset + span, :]
            g = gbuf[offset : offset + span, :]
            k = kvbuf[step, 0, :finish, :]
            v = kvbuf[step, 1, :finish, :]
            scores = lax.dot_general(q, k, NT, preferred_element_type=jnp.float32) * scaling
            places = lax.broadcasted_iota(jnp.int32, scores.shape, 0) + (base + offset)
            scores = jnp.where(
                lax.broadcasted_iota(jnp.int32, scores.shape, 1) <= places, scores, -jnp.inf
            )
            raised = jnp.exp(scores - jnp.max(scores, axis=-1, keepdims=True))
            weights = raised * (1.0 / jnp.sum(raised, axis=-1, keepdims=True))
            weights_bf = weights.astype(jnp.bfloat16)
            attention = jnp.dot(weights_bf, v, preferred_element_type=jnp.float32).astype(
                jnp.bfloat16
            )
            picked = marks[offset : offset + span, :] > 0.5
            zero = jnp.zeros_like(attention)
            obuf[offset : offset + span, :HEAD_SIZE] = jnp.where(picked, zero, attention)
            obuf[offset : offset + span, HEAD_SIZE:] = jnp.where(picked, attention, zero)
            delta = jnp.sum(
                g.astype(jnp.float32) * attention.astype(jnp.float32), axis=-1, keepdims=True
            )
            grad_weights = lax.dot_general(g, v, NT, preferred_element_type=jnp.float32)
            grad_scores = (weights * (grad_weights - delta) * scaling).astype(jnp.bfloat16)
            dq_buf[step, offset : offset + span, :] = jnp.dot(
                grad_scores, k, preferred_element_type=jnp.float32
            ).astype(jnp.bfloat16)
            dk = lax.dot_general(grad_scores, q, TN, preferred_element_type=jnp.float32)
            dv = lax.dot_general(weights_bf, g, TN, preferred_element_type=jnp.float32)
            if block == 1:
                dk_sum[:finish, :] = dk
                dv_sum[:finish, :] = dv
            else:
                dk_sum[:finish, :] += dk
                dv_sum[:finish, :] += dv
        dkv_buf[step, 0, : base + half, :] = dk_sum[: base + half, :].astype(jnp.bfloat16)
        dkv_buf[step, 1, : base + half, :] = dv_sum[: base + half, :].astype(jnp.bfloat16)
        width = total.shape[1]
        piece = min(512, width)
        for start in range(0, width, piece):
            total[:, start : start + piece] += jnp.dot(
                obuf[...], wbuf[step, :, start : start + piece], preferred_element_type=jnp.float32
            )

    def owner(lower):
        base = 0 if lower else half
        first = 0 if lower else blocks
        own_turn = 1 if lower else 0
        middle = {"ctx": (levels - 1 - place) * 2 + side}

        def pass_on(source, turn, beyond):
            remote(
                source, wbuf.at[turn * groups + 2], w_send.at[0, turn],
                w_sem.at[turn * groups + 2], {"fsdp": across},
            ).start()
            remote(
                source, wbuf.at[turn * groups + 1], w_send.at[1, turn],
                w_sem.at[turn * groups + 1], {"fsdp": partner},
            ).start()
            if beyond:
                remote(
                    source, wbuf.at[turn * groups], w_send.at[2, turn],
                    w_sem.at[turn * groups], middle,
                ).start()

        def relay(turn, beyond):
            slot = turn * groups
            arrived(wbuf.at[slot], w_sem.at[slot])
            pass_on(wbuf.at[slot], turn, beyond)

        def forward(step):
            arrived(kvbuf.at[step, :, pl.ds(0, half)], kv_sem.at[step])
            remote(
                kvbuf.at[step, :, pl.ds(0, half)], kvbuf.at[step, :, pl.ds(0, half)],
                lower_send.at[step], lower_sem.at[step], middle,
            ).start()

        def spread(buffer, skip, output, step, send_sem, receive_sem):
            cols = columns(step, side)
            for b in range(blocks):
                deliver(
                    buffer.at[pl.ds(skip + b * rows, rows)], output.at[:, cols],
                    send_sem, receive_sem, first + b,
                )

        def spread_keys(step):
            spread(dkv_buf.at[step, 0], base, dk_out, step, dkv_send.at[step], out_sem.at[2])
            spread(dkv_buf.at[step, 1], base, dv_out, step, dkv_send.at[step], out_sem.at[3])

        def finish_keys(step):
            arrived(dkv_buf.at[step, :, pl.ds(half, half)], rect_sem.at[step])
            for t in range(2):
                dkv_buf[step, t, :half, :] = (
                    dkv_buf[step, t, :half, :].astype(jnp.float32)
                    + dkv_buf[step, t, half:, :].astype(jnp.float32)
                ).astype(jnp.bfloat16)
            spread_keys(step)

        own_slot = wbuf.at[own_turn * groups]
        load = pltpu.make_async_copy(w_in, own_slot, w_sem.at[own_turn * groups])
        load.start()
        pass_on(w_in, own_turn, True)
        send_upstream()

        @pl.loop(0, steps)
        def _(step):
            send_step(step)

        total[...] = jnp.zeros_like(total)
        load.wait()
        if lower:
            forward(0)
            forward(1)
            relay(0, False)
            for step in range(2, AHEAD):
                forward(step)
        else:
            relay(1, False)
        arrived(up, single.at[1])
        arrived(marks, single.at[3])

        @pl.loop(0, steps)
        def _(step):
            if lower:
                @pl.when(step + AHEAD < steps)
                def _():
                    forward(step + AHEAD)

                @pl.when(step == 3)
                def _():
                    relay(2, True)

                @pl.when(step == 8)
                def _():
                    relay(3, False)

            else:
                @pl.when(step == 1)
                def _():
                    relay(3, True)

                @pl.when(step == 7)
                def _():
                    relay(2, False)

            turn, which = step // groups, step % groups

            @pl.when(which == 2)
            def _():
                arrived(wbuf.at[step], w_sem.at[step])
                remote(
                    wbuf.at[step], wbuf.at[step + 1], w_send.at[3, turn], w_sem.at[step + 1],
                    {"fsdp": partner},
                ).start()

            @pl.when(which % 2 == 1)
            def _():
                arrived(wbuf.at[step], w_sem.at[step])

            arrived(qbuf.at[step], q_sem.at[step])
            if not lower:
                arrived(kvbuf.at[step, :, pl.ds(half, half)], kv_sem.at[step])
                arrived(kvbuf.at[step, :, pl.ds(0, half)], lower_sem.at[step])
            compute(step, base)
            spread(dq_buf.at[step], 0, dq_out, step, dq_send.at[step], out_sem.at[1])
            if lower:
                @pl.when(step >= AHEAD)
                def _():
                    finish_keys(step - AHEAD)

            else:
                remote(
                    dkv_buf.at[step, :, pl.ds(0, half)], dkv_buf.at[step, :, pl.ds(half, half)],
                    rect_send.at[step], rect_sem.at[step], middle,
                ).start()
                spread_keys(step)

        leaf_row = 0 if lower else 1
        for b in (leaf_row, 1 - leaf_row):
            for s in range(2):
                @pl.when(side != s)
                def _():
                    start = (2 * b + s) * rows
                    part_out[b] = total[start : start + rows, :].astype(jnp.bfloat16)

            remote(
                part_out.at[b], part_in.at[b], part_send.at[b], part_sem.at[b],
                {"ctx": place * 2 + 1 - side},
            ).start()
        if lower:
            @pl.loop(steps - AHEAD, steps)
            def _(step):
                finish_keys(step)

        for b in (leaf_row, 1 - leaf_row):
            arrived(part_in.at[b], part_sem.at[b])
            for s in range(2):
                @pl.when(side == s)
                def _():
                    start = (2 * b + s) * rows
                    proj_buf[b] = (
                        total[start : start + rows, :] + part_in[b].astype(jnp.float32)
                    ).astype(jnp.bfloat16)

            if b == leaf_row:
                remote(
                    proj_buf.at[b], proj_out, single.at[4], out_sem.at[0],
                    {"ctx": (0 if lower else levels - 1) * 2 + side},
                ).start()
            else:
                pltpu.make_async_copy(proj_buf.at[b], proj_out, out_sem.at[0]).start()
        for b in range(2):
            sent(part_out.at[b], part_send.at[b])
        sent(proj_buf.at[leaf_row], single.at[4])
        sent(up.at[pl.ds(0, rows)], single.at[0])
        sent(marks.at[pl.ds(0, rows)], single.at[2])

        @pl.loop(0, levels)
        def _(turn):
            for kind in (0, 1, 3):
                sent(w_in, w_send.at[kind, turn])

        for turn in (1, 2) if lower else (0, 3):
            sent(w_in, w_send.at[2, turn])

        @pl.loop(0, steps)
        def _(step):
            sent(qbuf.at[step, pl.ds(0, 3 * rows)], in_send.at[step])
            sent(qbuf.at[step, pl.ds(0, 3 * rows)], dq_send.at[step])
            sent(kvbuf.at[step, :, pl.ds(0, 3 * rows)], dkv_send.at[step])
            if lower:
                sent(kvbuf.at[step, :, pl.ds(0, half)], lower_send.at[step])
            else:
                sent(kvbuf.at[step, :, pl.ds(0, half)], rect_send.at[step])

    @pl.when(place == 0)
    def _():
        leaf(True)

    @pl.when(place == levels - 1)
    def _():
        leaf(False)

    @pl.when(place == levels // 2 - 1)
    def _():
        owner(True)

    @pl.when(place == levels // 2)
    def _():
        owner(False)

    for i, output in enumerate((proj_out, dq_out, dk_out, dv_out)):
        arrived(output, out_sem.at[i])


def per_device(query_proj, key_proj, value_proj, modality, out_weight, grad_projected):
    size, groups = lax.axis_size("ctx"), lax.axis_size("fsdp")
    rows, width = query_proj.shape[1:]
    piece, out_width = out_weight.shape[1:]
    steps, half, length = groups * size // 2, rows * size // 2, rows * size
    marks = jnp.broadcast_to(modality[0][:, None], (rows, HEAD_SIZE)).astype(jnp.float32)
    bf, f32, dma = jnp.bfloat16, jnp.float32, pltpu.SemaphoreType.DMA
    results = pl.pallas_call(
        functools.partial(middle_kernel, groups, size),
        in_specs=[pl.BlockSpec(memory_space=pl.ANY)] * 6,
        out_specs=[pl.BlockSpec(memory_space=pl.ANY)] * 4,
        out_shape=[jax.ShapeDtypeStruct((rows, out_width), bf)]
        + [jax.ShapeDtypeStruct((rows, width), bf)] * 3,
        scratch_shapes=[
            pltpu.VMEM((steps, 2 * piece, out_width), bf),
            pltpu.VMEM((steps, 2, length, HEAD_SIZE), bf),
            pltpu.VMEM((steps, half, HEAD_SIZE), bf),
            pltpu.VMEM((half, out_width), bf),
            pltpu.VMEM((half, HEAD_SIZE), f32),
            pltpu.VMEM((half, out_width), f32),
            pltpu.VMEM((half, HEAD_SIZE), bf),
            pltpu.VMEM((half, 2 * HEAD_SIZE), bf),
            pltpu.VMEM((steps, half, HEAD_SIZE), bf),
            pltpu.VMEM((steps, 2, length, HEAD_SIZE), bf),
            pltpu.VMEM((length, HEAD_SIZE), f32),
            pltpu.VMEM((length, HEAD_SIZE), f32),
            pltpu.VMEM((2, rows, out_width), bf),
            pltpu.VMEM((2, rows, out_width), bf),
            pltpu.VMEM((2, rows, out_width), bf),
        ]
        + [dma((steps,))] * 10
        + [dma((4, size // 2)), dma((5,)), dma((4,)), dma((2,)), dma((2,))],
        compiler_params=pltpu.CompilerParams(
            collective_id=0, has_side_effects=True, vmem_limit_bytes=67043328
        ),
    )(
        query_proj[0],
        key_proj[0],
        value_proj[0],
        out_weight.reshape(2 * piece, out_width),
        grad_projected[0],
        marks,
    )
    return tuple(a[None] for a in results)


def aligned(mesh, query_shape, weight_shape):
    groups, size = mesh.shape["fsdp"], mesh.shape["ctx"]
    return (
        groups == 4
        and size == 8
        and weight_shape[1] == groups * size * HEAD_SIZE
        and query_shape[0] == groups
        and query_shape[1] <= 1024
    )


def solution(mesh):
    placed = (
        P("fsdp", "ctx", None),
        P("fsdp", "ctx", None),
        P("fsdp", "ctx", None),
        P("fsdp", "ctx"),
        P(None, ("fsdp", "ctx"), None),
        P("fsdp", "ctx", None),
    )
    def whole(*arrays):
        local = per_device if aligned(mesh, arrays[0].shape, arrays[4].shape) else per_device_gathered
        return jax.shard_map(
            local,
            mesh=mesh,
            in_specs=placed,
            out_specs=(P("fsdp", "ctx", None),) * 4,
            check_vma=False,
        )(*arrays)

    return whole
```

```python
import functools

import jax
import jax.numpy as jnp
from jax import lax
from jax.experimental import pallas as pl
from jax.experimental.pallas import tpu as pltpu
from jax.sharding import PartitionSpec as P

HEAD_SIZE = 128


def block_count(length):
    return max(1, min(8, length // 512))


def probabilities(query_block, key_prefix, offset):
    scaling = query_block.shape[-1] ** (-0.5)
    scores = (
        jnp.einsum("hqd,hkd->hqk", query_block, key_prefix, preferred_element_type=jnp.float32)
        * scaling
    )
    query_places = offset + jnp.arange(query_block.shape[1])
    key_places = jnp.arange(key_prefix.shape[1])
    scores = jnp.where(key_places[None, None, :] <= query_places[None, :, None], scores, -jnp.inf)
    highest = jnp.max(scores, axis=-1, keepdims=True)
    raised = jnp.exp(scores - highest)
    return raised / jnp.sum(raised, axis=-1, keepdims=True)


def attend_forward(queries, keys_all, values_all):
    length = queries.shape[1]
    block_rows = length // block_count(length)
    pieces = []
    for block_index in range(length // block_rows):
        offset = block_index * block_rows
        finish = offset + block_rows
        weights = probabilities(queries[:, offset:finish], keys_all[:, :finish], offset).astype(
            jnp.bfloat16
        )
        output = jnp.einsum(
            "hqk,hkd->hqd", weights, values_all[:, :finish], preferred_element_type=jnp.float32
        )
        pieces.append(output.astype(jnp.bfloat16))
    return jnp.concatenate(pieces, axis=1)


def attend_backward(queries, keys_all, values_all, attention, grad_attention):
    length = queries.shape[1]
    block_rows = length // block_count(length)
    scaling = queries.shape[-1] ** (-0.5)
    grad_keys = jnp.zeros(queries.shape, jnp.float32)
    grad_values = jnp.zeros(queries.shape, jnp.float32)
    query_pieces = []
    for block_index in range(length // block_rows):
        offset = block_index * block_rows
        finish = offset + block_rows
        query_block = queries[:, offset:finish]
        weights = probabilities(query_block, keys_all[:, :finish], offset)
        grad_block = grad_attention[:, offset:finish]
        attn_block = attention[:, offset:finish]
        grad_values = grad_values.at[:, :finish].add(
            jnp.einsum(
                "hqk,hqd->hkd",
                weights.astype(jnp.bfloat16),
                grad_block,
                preferred_element_type=jnp.float32,
            )
        )
        grad_weights = jnp.einsum(
            "hqd,hkd->hqk", grad_block, values_all[:, :finish], preferred_element_type=jnp.float32
        )
        row_delta = jnp.sum(
            grad_block.astype(jnp.float32) * attn_block.astype(jnp.float32), axis=-1, keepdims=True
        )
        grad_scores = (weights * (grad_weights - row_delta) * scaling).astype(jnp.bfloat16)
        query_pieces.append(
            jnp.einsum(
                "hqk,hkd->hqd",
                grad_scores,
                keys_all[:, :finish],
                preferred_element_type=jnp.float32,
            ).astype(jnp.bfloat16)
        )
        grad_keys = grad_keys.at[:, :finish].add(
            jnp.einsum("hqk,hqd->hkd", grad_scores, query_block, preferred_element_type=jnp.float32)
        )
    return (
        jnp.concatenate(query_pieces, axis=1),
        grad_keys.astype(jnp.bfloat16),
        grad_values.astype(jnp.bfloat16),
    )


def transposed_product(left, right):
    return lax.dot_general(
        left, right, (((1,), (1,)), ((), ())), preferred_element_type=jnp.float32
    )


def heads_first(flat, length, local_heads):
    return flat.reshape(length, local_heads, HEAD_SIZE).transpose(1, 0, 2)


def heads_last(stacked, length, local_width):
    return stacked.transpose(1, 0, 2).reshape(1, length, local_width)


def per_device_gathered(query_proj, key_proj, value_proj, modality, out_weight, grad_projected):
    context_size = lax.axis_size("ctx")
    row_count = query_proj.shape[1]
    inner_width = query_proj.shape[2]
    length = row_count * context_size
    local_width = inner_width // context_size
    local_heads = local_width // HEAD_SIZE
    head_query, head_key, head_value = (
        lax.all_to_all(query_proj, "ctx", split_axis=2, concat_axis=1, tiled=True),
        lax.all_to_all(key_proj, "ctx", split_axis=2, concat_axis=1, tiled=True),
        lax.all_to_all(value_proj, "ctx", split_axis=2, concat_axis=1, tiled=True),
    )
    head_query = heads_first(head_query, length, local_heads)
    head_key = heads_first(head_key, length, local_heads)
    head_value = heads_first(head_value, length, local_heads)
    attention = attend_forward(head_query, head_key, head_value)
    sending = heads_last(attention, length, local_width)
    attn_rows = lax.all_to_all(sending, "ctx", split_axis=1, concat_axis=2, tiled=True)[0]
    upstream = grad_projected[0]
    weight_piece = lax.all_gather(out_weight, ("fsdp", "ctx"), axis=1, tiled=True)
    text_out = jnp.dot(attn_rows, weight_piece[0], preferred_element_type=jnp.float32)
    image_out = jnp.dot(attn_rows, weight_piece[1], preferred_element_type=jnp.float32)
    text_grad = transposed_product(upstream, weight_piece[0])
    image_grad = transposed_product(upstream, weight_piece[1])
    text_out, image_out, text_grad, image_grad = (text_out, image_out, text_grad, image_grad)
    image_rows = (modality[0] == 1)[:, None]
    projected = jnp.where(image_rows, image_out, text_out).astype(jnp.bfloat16)[None]
    grad_rows = jnp.where(image_rows, image_grad, text_grad).astype(jnp.bfloat16)
    grad_heads = lax.all_to_all(grad_rows[None], "ctx", split_axis=2, concat_axis=1, tiled=True)
    grad_heads = heads_first(grad_heads, length, local_heads)
    grad_q, grad_k, grad_v = attend_backward(
        head_query, head_key, head_value, attention, grad_heads
    )
    grad_query, grad_key, grad_value = (
        lax.all_to_all(
            heads_last(grad_q, length, local_width), "ctx", split_axis=1, concat_axis=2, tiled=True
        ),
        lax.all_to_all(
            heads_last(grad_k, length, local_width), "ctx", split_axis=1, concat_axis=2, tiled=True
        ),
        lax.all_to_all(
            heads_last(grad_v, length, local_width), "ctx", split_axis=1, concat_axis=2, tiled=True
        ),
    )
    return (projected, grad_query, grad_key, grad_value)


NT = (((1,), (1,)), ((), ()))
TN = (((0,), (0,)), ((), ()))
AHEAD = 4
BEHIND = 2
LOWER_SPLIT = 6
CHUNKS = 8


def middle_kernel(
    groups,
    size,
    q_in, k_in, v_in, w_in, up_in, mark_in,
    proj_out, dq_out, dk_out, dv_out,
    wbuf, kvbuf, qbuf, up, tags, marks, total, gbuf, obuf, dq_buf, dkv_buf, dk_sum, dv_sum,
    part_out, part_in, proj_buf,
    kv_sem, q_sem, lower_sem, rect_sem, w_sem, chunk_sem,
    in_send, lower_send, rect_send, dq_send, dkv_send, w_send,
    single, out_sem, part_send, part_sem,
):
    rows = q_in.shape[0]
    levels = size // 2
    steps = groups * levels
    blocks = size // 2
    half = blocks * rows
    scaling = HEAD_SIZE ** (-0.5)
    group, ctx = lax.axis_index("fsdp"), lax.axis_index("ctx")
    place, side = ctx // 2, ctx % 2
    owner_place = levels // 2 - 1 + place // (levels // 2)
    across = (group + 2) % groups
    partner = group + 1 - 2 * (group % 2)
    position = ctx % blocks

    def halves(lower):
        split = LOWER_SPLIT * rows // 8 if lower else rows // 2
        return split, pl.ds(0, split), pl.ds(split, rows - split)

    def columns(step, p):
        turn, which = step // groups, step % groups
        late = turn // 2
        source = (1 - late) * (2 - turn) + late * 3 * (3 - turn)
        owner = ((group // 2 + which // 2) % 2) * 2 + (group % 2 + which % 2) % 2
        head = owner * size + 2 * source + p
        return pl.ds(pl.multiple_of(head * HEAD_SIZE, HEAD_SIZE), HEAD_SIZE)

    def remote(source, target, send_sem, receive_sem, device):
        return pltpu.make_async_remote_copy(
            src_ref=source,
            dst_ref=target,
            send_sem=send_sem,
            recv_sem=receive_sem,
            device_id=device,
            device_id_type=pl.DeviceIdType.MESH,
        )

    def arrived(ref, sem):
        remote(ref, ref, sem, sem, {"ctx": (ctx + 1) % size}).wait_recv()

    def sent(ref, sem):
        remote(ref, ref, sem, sem, {"ctx": (ctx + 1) % size}).wait_send()

    def deliver(source, target, send_sem, receive_sem, to):
        @pl.when(to == ctx)
        def _():
            pltpu.make_async_copy(source, target, receive_sem).start()

        @pl.when(to != ctx)
        def _():
            remote(source, target, send_sem, receive_sem, {"ctx": to}).start()

    barrier = pltpu.get_barrier_semaphore()
    greeted = [{"ctx": lax.rem(ctx + step, size)} for step in range(1, size)]
    greeted += [{"fsdp": across}, {"fsdp": partner}]
    for peer in greeted:
        pl.semaphore_signal(barrier, 1, device_id=peer, device_id_type=pl.DeviceIdType.MESH)
    pl.semaphore_wait(barrier, len(greeted))

    own_rows = pl.ds(pl.multiple_of(position * rows, rows), rows)
    key_rows = pl.ds(pl.multiple_of(ctx * rows, rows), rows)

    def piece(chunk):
        size_of = w_in.shape[0] // CHUNKS
        return pl.ds(pl.multiple_of(chunk * size_of, size_of), size_of)

    def send_upstream():
        for p in range(2):
            to = owner_place * 2 + p
            deliver(up_in, up.at[own_rows], single.at[0], single.at[1], to)
            deliver(mark_in, tags.at[position], single.at[2], single.at[3], to)

    def send_step(step):
        for p in range(2):
            to, cols = owner_place * 2 + p, columns(step, p)
            deliver(k_in.at[:, cols], kvbuf.at[step, 0, key_rows], in_send.at[step], kv_sem.at[step], to)
            deliver(v_in.at[:, cols], kvbuf.at[step, 1, key_rows], in_send.at[step], kv_sem.at[step], to)
            deliver(q_in.at[:, cols], qbuf.at[step, own_rows], in_send.at[step], q_sem.at[step], to)

    def leaf(lower):
        split, first_rows, rest = halves(lower)
        turn, opening = (3, 4) if lower else (2, 1)

        def send_piece(chunk):
            remote(
                w_in.at[piece(chunk)], wbuf.at[turn * groups, piece(chunk)],
                w_send.at[0, 0], chunk_sem.at[turn, chunk],
                {"ctx": owner_place * 2 + side},
            ).start()

        if not lower:
            @pl.loop(0, CHUNKS)
            def _(chunk):
                send_piece(chunk)

        @pl.loop(0, steps)
        def _(step):
            @pl.when(step == opening)
            def _():
                send_upstream()

            if lower:
                @pl.when((step >= 1) & (step <= CHUNKS))
                def _():
                    send_piece(step - 1)

            send_step(step)

        arrived(part_in.at[1, rest], part_sem.at[1])
        arrived(part_in.at[2, rest], part_sem.at[2])
        proj_buf[0, rest] = (
            part_in[1, rest].astype(jnp.float32) + part_in[2, rest].astype(jnp.float32)
        ).astype(jnp.bfloat16)
        pltpu.make_async_copy(proj_buf.at[0, rest], proj_out.at[rest], out_sem.at[0]).start()
        sent(w_in, w_send.at[0, 0])
        sent(up.at[pl.ds(0, 2 * rows)], single.at[0])
        sent(tags.at[pl.ds(0, 2)], single.at[2])

        @pl.loop(0, steps)
        def _(step):
            sent(kvbuf.at[step, :, pl.ds(0, 3 * rows)], in_send.at[step])

    def compute(step, base, between=None):
        both = lax.dot_general(up[...], wbuf[step], NT, preferred_element_type=jnp.float32)
        image = marks[...] > 0.5
        gbuf[...] = jnp.where(image, both[:, HEAD_SIZE:], both[:, :HEAD_SIZE]).astype(jnp.bfloat16)
        span = half // 2
        kept = []
        for block in range(2):
            offset = block * span
            finish = base + offset + span
            q = qbuf[step, offset : offset + span, :]
            k = kvbuf[step, 0, :finish, :]
            v = kvbuf[step, 1, :finish, :]
            scores = lax.dot_general(q, k, NT, preferred_element_type=jnp.float32) * scaling
            places = lax.broadcasted_iota(jnp.int32, scores.shape, 0) + (base + offset)
            scores = jnp.where(
                lax.broadcasted_iota(jnp.int32, scores.shape, 1) <= places, scores, -jnp.inf
            )
            raised = jnp.exp(scores - jnp.max(scores, axis=-1, keepdims=True))
            weights = raised * (1.0 / jnp.sum(raised, axis=-1, keepdims=True))
            attention = jnp.dot(
                weights.astype(jnp.bfloat16), v, preferred_element_type=jnp.float32
            ).astype(jnp.bfloat16)
            picked = marks[offset : offset + span, :] > 0.5
            zero = jnp.zeros_like(attention)
            obuf[offset : offset + span, :HEAD_SIZE] = jnp.where(picked, zero, attention)
            obuf[offset : offset + span, HEAD_SIZE:] = jnp.where(picked, attention, zero)
            kept.append((weights, attention))
        width = total.shape[1]
        wide = min(512, width)
        for start in range(0, width, wide):
            total[:, start : start + wide] += jnp.dot(
                obuf[...], wbuf[step, :, start : start + wide], preferred_element_type=jnp.float32
            )
        if between is not None:
            between()
        for block in reversed(range(2)):
            offset = block * span
            finish = base + offset + span
            q = qbuf[step, offset : offset + span, :]
            g = gbuf[offset : offset + span, :]
            k = kvbuf[step, 0, :finish, :]
            v = kvbuf[step, 1, :finish, :]
            weights, attention = kept[block]
            delta = jnp.sum(
                g.astype(jnp.float32) * attention.astype(jnp.float32), axis=-1, keepdims=True
            )
            grad_weights = lax.dot_general(g, v, NT, preferred_element_type=jnp.float32)
            grad_scores = (weights * (grad_weights - delta) * scaling).astype(jnp.bfloat16)
            dq_buf[step, offset : offset + span, :] = jnp.dot(
                grad_scores, k, preferred_element_type=jnp.float32
            ).astype(jnp.bfloat16)
            dk = lax.dot_general(grad_scores, q, TN, preferred_element_type=jnp.float32)
            dv = lax.dot_general(
                weights.astype(jnp.bfloat16), g, TN, preferred_element_type=jnp.float32
            )
            if block == 1:
                dk_sum[:finish, :] = dk
                dv_sum[:finish, :] = dv
            else:
                dk_sum[:finish, :] += dk
                dv_sum[:finish, :] += dv
        dkv_buf[step, 0, : base + half, :] = dk_sum[: base + half, :].astype(jnp.bfloat16)
        dkv_buf[step, 1, : base + half, :] = dv_sum[: base + half, :].astype(jnp.bfloat16)

    def owner(lower):
        base = 0 if lower else half
        first = 0 if lower else blocks
        own_turn = 1 if lower else 0
        middle = {"ctx": (levels - 1 - place) * 2 + side}

        def pass_on(source, turn, part, beyond):
            slot = turn * groups
            remote(
                source, wbuf.at[slot + 2, part], w_send.at[0, turn], w_sem.at[slot + 2],
                {"fsdp": across},
            ).start()
            remote(
                source, wbuf.at[slot + 1, part], w_send.at[1, turn], w_sem.at[slot + 1],
                {"fsdp": partner},
            ).start()
            if beyond is not None:
                remote(
                    source, wbuf.at[slot, part], w_send.at[2, turn], beyond, middle,
                ).start()

        def relay(turn, chunk, beyond):
            part = piece(chunk)
            source = wbuf.at[turn * groups, part]
            arrived(source, chunk_sem.at[turn, chunk])
            pass_on(source, turn, part, chunk_sem.at[turn, chunk] if beyond else None)

        def forward(step):
            arrived(kvbuf.at[step, :, pl.ds(0, half)], kv_sem.at[step])
            remote(
                kvbuf.at[step, :, pl.ds(0, half)], kvbuf.at[step, :, pl.ds(0, half)],
                lower_send.at[step], lower_sem.at[step], middle,
            ).start()

            @pl.when((step >= 1) & (step <= CHUNKS))
            def _():
                relay(3, step - 1, True)

        def spread(buffer, skip, output, step, send_sem, receive_sem):
            cols = columns(step, side)
            for b in range(blocks):
                deliver(
                    buffer.at[pl.ds(skip + b * rows, rows)], output.at[:, cols],
                    send_sem, receive_sem, first + b,
                )

        def spread_keys(step):
            spread(dkv_buf.at[step, 0], base, dk_out, step, dkv_send.at[step], out_sem.at[2])
            spread(dkv_buf.at[step, 1], base, dv_out, step, dkv_send.at[step], out_sem.at[3])

        def finish_keys(step):
            arrived(dkv_buf.at[step, :, pl.ds(half, half)], rect_sem.at[step])
            for t in range(2):
                dkv_buf[step, t, :half, :] = (
                    dkv_buf[step, t, :half, :].astype(jnp.float32)
                    + dkv_buf[step, t, half:, :].astype(jnp.float32)
                ).astype(jnp.bfloat16)
            spread_keys(step)

        own_slot = wbuf.at[own_turn * groups]
        load = pltpu.make_async_copy(w_in, own_slot, w_sem.at[own_turn * groups])
        load.start()

        @pl.loop(0, CHUNKS)
        def _(chunk):
            part = piece(chunk)
            pass_on(w_in.at[part], own_turn, part, chunk_sem.at[own_turn, chunk])

        send_upstream()

        @pl.loop(0, steps)
        def _(step):
            send_step(step)

        total[...] = jnp.zeros_like(total)
        load.wait()

        @pl.loop(0, CHUNKS)
        def _(chunk):
            relay(1 - own_turn, chunk, False)
            if not lower:
                relay(2, chunk, True)

        if lower:
            @pl.loop(0, AHEAD)
            def _(step):
                forward(step)

        arrived(up, single.at[1])
        arrived(tags, single.at[3])
        for b in range(blocks):
            wide = jnp.broadcast_to(tags[b].astype(jnp.float32), (HEAD_SIZE, rows))
            marks[b * rows : (b + 1) * rows, :] = wide.T

        def advance(step, between=None):
            if lower:
                @pl.when(step + AHEAD < steps)
                def _():
                    forward(step + AHEAD)

                @pl.when(step == 1)
                def _():
                    @pl.loop(0, CHUNKS)
                    def _(chunk):
                        relay(2, chunk, False)

            turn, which = step // groups, step % groups

            @pl.when(which == 2)
            def _():
                arrived(wbuf.at[step], w_sem.at[step])
                remote(
                    wbuf.at[step], wbuf.at[step + 1], w_send.at[3, turn], w_sem.at[step + 1],
                    {"fsdp": partner},
                ).start()

            @pl.when(which % 2 == 1)
            def _():
                arrived(wbuf.at[step], w_sem.at[step])

            arrived(qbuf.at[step], q_sem.at[step])
            if not lower:
                arrived(kvbuf.at[step, :, pl.ds(half, half)], kv_sem.at[step])
                arrived(kvbuf.at[step, :, pl.ds(0, half)], lower_sem.at[step])

                @pl.when((step >= 2) & (step < 2 + CHUNKS))
                def _():
                    relay(3, step - 2, False)

            compute(step, base, between)
            spread(dq_buf.at[step], 0, dq_out, step, dq_send.at[step], out_sem.at[1])
            if lower:
                @pl.when(step >= BEHIND)
                def _():
                    finish_keys(step - BEHIND)

            else:
                remote(
                    dkv_buf.at[step, :, pl.ds(0, half)], dkv_buf.at[step, :, pl.ds(half, half)],
                    rect_send.at[step], rect_sem.at[step], middle,
                ).start()
                spread_keys(step)

        split, first_rows, rest = halves(lower)
        leaf_row = 0 if lower else 1
        near_row = 1 - leaf_row
        end_place = 0 if lower else levels - 1
        other = {"ctx": place * 2 + 1 - side}

        def exchange_parts():
            for s in range(2):
                @pl.when(side != s)
                def _():
                    start = (2 * leaf_row + s) * rows
                    part_out[0] = total[start : start + rows, :].astype(jnp.bfloat16)

                @pl.when(side == s)
                def _():
                    start = (2 * leaf_row + s) * rows + split
                    part_out[2, rest] = total[start : start + rows - split, :].astype(
                        jnp.bfloat16
                    )

            remote(
                part_out.at[0, rest], part_in.at[1, rest], part_send.at[1], part_sem.at[1],
                {"ctx": end_place * 2 + 1 - side},
            ).start()
            remote(
                part_out.at[0, first_rows], part_in.at[0, first_rows], part_send.at[0],
                part_sem.at[0], other,
            ).start()
            remote(
                part_out.at[2, rest], part_in.at[2, rest], part_send.at[2], part_sem.at[2],
                {"ctx": end_place * 2 + side},
            ).start()
            for s in range(2):
                @pl.when(side != s)
                def _():
                    start = (2 * near_row + s) * rows
                    part_out[1] = total[start : start + rows, :].astype(jnp.bfloat16)

            remote(
                part_out.at[1], part_in.at[1], part_send.at[3], part_sem.at[3], other
            ).start()

        @pl.loop(0, steps - 1)
        def _(step):
            advance(step)

        advance(steps - 1, exchange_parts)
        if lower:
            @pl.loop(steps - BEHIND, steps - 2)
            def _(step):
                finish_keys(step)

        arrived(part_in.at[0, first_rows], part_sem.at[0])
        for s in range(2):
            @pl.when(side == s)
            def _():
                start = (2 * leaf_row + s) * rows
                proj_buf[0, first_rows] = (
                    total[start : start + split, :] + part_in[0, first_rows].astype(jnp.float32)
                ).astype(jnp.bfloat16)

        remote(
            proj_buf.at[0, first_rows], proj_out.at[first_rows], single.at[4], out_sem.at[0],
            {"ctx": end_place * 2 + side},
        ).start()
        if lower:
            @pl.loop(steps - 2, steps)
            def _(step):
                finish_keys(step)

        arrived(part_in.at[1], part_sem.at[3])
        for s in range(2):
            @pl.when(side == s)
            def _():
                start = (2 * near_row + s) * rows
                proj_buf[1] = (
                    total[start : start + rows, :] + part_in[1].astype(jnp.float32)
                ).astype(jnp.bfloat16)

        pltpu.make_async_copy(proj_buf.at[1], proj_out, out_sem.at[0]).start()
        sent(part_out.at[0, first_rows], part_send.at[0])
        sent(part_out.at[0, rest], part_send.at[1])
        sent(part_out.at[0, rest], part_send.at[2])
        sent(part_out.at[1], part_send.at[3])
        sent(proj_buf.at[0, first_rows], single.at[4])
        sent(up.at[pl.ds(0, rows)], single.at[0])
        sent(tags.at[pl.ds(0, 1)], single.at[2])

        @pl.loop(0, levels)
        def _(turn):
            for kind in (0, 1, 3):
                sent(w_in, w_send.at[kind, turn])

        for turn in (1, 3) if lower else (0, 2):
            sent(w_in, w_send.at[2, turn])

        @pl.loop(0, steps)
        def _(step):
            sent(qbuf.at[step, pl.ds(0, 3 * rows)], in_send.at[step])
            sent(qbuf.at[step, pl.ds(0, 3 * rows)], dq_send.at[step])
            sent(kvbuf.at[step, :, pl.ds(0, 3 * rows)], dkv_send.at[step])
            if lower:
                sent(kvbuf.at[step, :, pl.ds(0, half)], lower_send.at[step])
            else:
                sent(kvbuf.at[step, :, pl.ds(0, half)], rect_send.at[step])

    @pl.when(place == 0)
    def _():
        leaf(True)

    @pl.when(place == levels - 1)
    def _():
        leaf(False)

    @pl.when(place == levels // 2 - 1)
    def _():
        owner(True)

    @pl.when(place == levels // 2)
    def _():
        owner(False)

    for i, output in enumerate((proj_out, dq_out, dk_out, dv_out)):
        arrived(output, out_sem.at[i])


def per_device(query_proj, key_proj, value_proj, modality, out_weight, grad_projected):
    size, groups = lax.axis_size("ctx"), lax.axis_size("fsdp")
    rows, width = query_proj.shape[1:]
    piece, out_width = out_weight.shape[1:]
    steps, half, length = groups * size // 2, rows * size // 2, rows * size
    bf, f32, dma = jnp.bfloat16, jnp.float32, pltpu.SemaphoreType.DMA
    results = pl.pallas_call(
        functools.partial(middle_kernel, groups, size),
        in_specs=[pl.BlockSpec(memory_space=pl.ANY)] * 6,
        out_specs=[pl.BlockSpec(memory_space=pl.ANY)] * 4,
        out_shape=[jax.ShapeDtypeStruct((rows, out_width), bf)]
        + [jax.ShapeDtypeStruct((rows, width), bf)] * 3,
        scratch_shapes=[
            pltpu.VMEM((steps, 2 * piece, out_width), bf),
            pltpu.VMEM((steps, 2, length, HEAD_SIZE), bf),
            pltpu.VMEM((steps, half, HEAD_SIZE), bf),
            pltpu.VMEM((half, out_width), bf),
            pltpu.VMEM((size // 2, 1, rows), jnp.int32),
            pltpu.VMEM((half, HEAD_SIZE), f32),
            pltpu.VMEM((half, out_width), f32),
            pltpu.VMEM((half, HEAD_SIZE), bf),
            pltpu.VMEM((half, 2 * HEAD_SIZE), bf),
            pltpu.VMEM((steps, half, HEAD_SIZE), bf),
            pltpu.VMEM((steps, 2, length, HEAD_SIZE), bf),
            pltpu.VMEM((length, HEAD_SIZE), f32),
            pltpu.VMEM((length, HEAD_SIZE), f32),
            pltpu.VMEM((3, rows, out_width), bf),
            pltpu.VMEM((3, rows, out_width), bf),
            pltpu.VMEM((2, rows, out_width), bf),
        ]
        + [dma((steps,))] * 5
        + [dma((size // 2, CHUNKS))]
        + [dma((steps,))] * 5
        + [dma((4, size // 2)), dma((5,)), dma((4,)), dma((4,)), dma((4,))],
        compiler_params=pltpu.CompilerParams(
            collective_id=0, has_side_effects=True, vmem_limit_bytes=67043328
        ),
    )(
        query_proj[0],
        key_proj[0],
        value_proj[0],
        out_weight.reshape(2 * piece, out_width),
        grad_projected[0],
        modality,
    )
    return tuple(a[None] for a in results)


def aligned(mesh, query_shape, weight_shape):
    groups, size = mesh.shape["fsdp"], mesh.shape["ctx"]
    return (
        groups == 4
        and size == 8
        and weight_shape[1] == groups * size * HEAD_SIZE
        and query_shape[0] == groups
        and query_shape[1] <= 1024
    )


def solution(mesh):
    placed = (
        P("fsdp", "ctx", None),
        P("fsdp", "ctx", None),
        P("fsdp", "ctx", None),
        P("fsdp", "ctx"),
        P(None, ("fsdp", "ctx"), None),
        P("fsdp", "ctx", None),
    )
    def whole(*arrays):
        local = per_device if aligned(mesh, arrays[0].shape, arrays[4].shape) else per_device_gathered
        return jax.shard_map(
            local,
            mesh=mesh,
            in_specs=placed,
            out_specs=(P("fsdp", "ctx", None),) * 4,
            check_vma=False,
        )(*arrays)

    return whole
```

```python
import functools

import jax
import jax.numpy as jnp
from jax import lax
from jax.experimental import pallas as pl
from jax.experimental.pallas import tpu as pltpu
from jax.sharding import PartitionSpec as P

HEAD_SIZE = 128


def block_count(length):
    return max(1, min(8, length // 512))


def probabilities(query_block, key_prefix, offset):
    scaling = query_block.shape[-1] ** (-0.5)
    scores = (
        jnp.einsum("hqd,hkd->hqk", query_block, key_prefix, preferred_element_type=jnp.float32)
        * scaling
    )
    query_places = offset + jnp.arange(query_block.shape[1])
    key_places = jnp.arange(key_prefix.shape[1])
    scores = jnp.where(key_places[None, None, :] <= query_places[None, :, None], scores, -jnp.inf)
    highest = jnp.max(scores, axis=-1, keepdims=True)
    raised = jnp.exp(scores - highest)
    return raised / jnp.sum(raised, axis=-1, keepdims=True)


def attend_forward(queries, keys_all, values_all):
    length = queries.shape[1]
    block_rows = length // block_count(length)
    pieces = []
    for block_index in range(length // block_rows):
        offset = block_index * block_rows
        finish = offset + block_rows
        weights = probabilities(queries[:, offset:finish], keys_all[:, :finish], offset).astype(
            jnp.bfloat16
        )
        output = jnp.einsum(
            "hqk,hkd->hqd", weights, values_all[:, :finish], preferred_element_type=jnp.float32
        )
        pieces.append(output.astype(jnp.bfloat16))
    return jnp.concatenate(pieces, axis=1)


def attend_backward(queries, keys_all, values_all, attention, grad_attention):
    length = queries.shape[1]
    block_rows = length // block_count(length)
    scaling = queries.shape[-1] ** (-0.5)
    grad_keys = jnp.zeros(queries.shape, jnp.float32)
    grad_values = jnp.zeros(queries.shape, jnp.float32)
    query_pieces = []
    for block_index in range(length // block_rows):
        offset = block_index * block_rows
        finish = offset + block_rows
        query_block = queries[:, offset:finish]
        weights = probabilities(query_block, keys_all[:, :finish], offset)
        grad_block = grad_attention[:, offset:finish]
        attn_block = attention[:, offset:finish]
        grad_values = grad_values.at[:, :finish].add(
            jnp.einsum(
                "hqk,hqd->hkd",
                weights.astype(jnp.bfloat16),
                grad_block,
                preferred_element_type=jnp.float32,
            )
        )
        grad_weights = jnp.einsum(
            "hqd,hkd->hqk", grad_block, values_all[:, :finish], preferred_element_type=jnp.float32
        )
        row_delta = jnp.sum(
            grad_block.astype(jnp.float32) * attn_block.astype(jnp.float32), axis=-1, keepdims=True
        )
        grad_scores = (weights * (grad_weights - row_delta) * scaling).astype(jnp.bfloat16)
        query_pieces.append(
            jnp.einsum(
                "hqk,hkd->hqd",
                grad_scores,
                keys_all[:, :finish],
                preferred_element_type=jnp.float32,
            ).astype(jnp.bfloat16)
        )
        grad_keys = grad_keys.at[:, :finish].add(
            jnp.einsum("hqk,hqd->hkd", grad_scores, query_block, preferred_element_type=jnp.float32)
        )
    return (
        jnp.concatenate(query_pieces, axis=1),
        grad_keys.astype(jnp.bfloat16),
        grad_values.astype(jnp.bfloat16),
    )


def transposed_product(left, right):
    return lax.dot_general(
        left, right, (((1,), (1,)), ((), ())), preferred_element_type=jnp.float32
    )


def heads_first(flat, length, local_heads):
    return flat.reshape(length, local_heads, HEAD_SIZE).transpose(1, 0, 2)


def heads_last(stacked, length, local_width):
    return stacked.transpose(1, 0, 2).reshape(1, length, local_width)


def per_device_gathered(query_proj, key_proj, value_proj, modality, out_weight, grad_projected):
    context_size = lax.axis_size("ctx")
    row_count = query_proj.shape[1]
    inner_width = query_proj.shape[2]
    length = row_count * context_size
    local_width = inner_width // context_size
    local_heads = local_width // HEAD_SIZE
    head_query, head_key, head_value = (
        lax.all_to_all(query_proj, "ctx", split_axis=2, concat_axis=1, tiled=True),
        lax.all_to_all(key_proj, "ctx", split_axis=2, concat_axis=1, tiled=True),
        lax.all_to_all(value_proj, "ctx", split_axis=2, concat_axis=1, tiled=True),
    )
    head_query = heads_first(head_query, length, local_heads)
    head_key = heads_first(head_key, length, local_heads)
    head_value = heads_first(head_value, length, local_heads)
    attention = attend_forward(head_query, head_key, head_value)
    sending = heads_last(attention, length, local_width)
    attn_rows = lax.all_to_all(sending, "ctx", split_axis=1, concat_axis=2, tiled=True)[0]
    upstream = grad_projected[0]
    weight_piece = lax.all_gather(out_weight, ("fsdp", "ctx"), axis=1, tiled=True)
    text_out = jnp.dot(attn_rows, weight_piece[0], preferred_element_type=jnp.float32)
    image_out = jnp.dot(attn_rows, weight_piece[1], preferred_element_type=jnp.float32)
    text_grad = transposed_product(upstream, weight_piece[0])
    image_grad = transposed_product(upstream, weight_piece[1])
    text_out, image_out, text_grad, image_grad = (text_out, image_out, text_grad, image_grad)
    image_rows = (modality[0] == 1)[:, None]
    projected = jnp.where(image_rows, image_out, text_out).astype(jnp.bfloat16)[None]
    grad_rows = jnp.where(image_rows, image_grad, text_grad).astype(jnp.bfloat16)
    grad_heads = lax.all_to_all(grad_rows[None], "ctx", split_axis=2, concat_axis=1, tiled=True)
    grad_heads = heads_first(grad_heads, length, local_heads)
    grad_q, grad_k, grad_v = attend_backward(
        head_query, head_key, head_value, attention, grad_heads
    )
    grad_query, grad_key, grad_value = (
        lax.all_to_all(
            heads_last(grad_q, length, local_width), "ctx", split_axis=1, concat_axis=2, tiled=True
        ),
        lax.all_to_all(
            heads_last(grad_k, length, local_width), "ctx", split_axis=1, concat_axis=2, tiled=True
        ),
        lax.all_to_all(
            heads_last(grad_v, length, local_width), "ctx", split_axis=1, concat_axis=2, tiled=True
        ),
    )
    return (projected, grad_query, grad_key, grad_value)


NT = (((1,), (1,)), ((), ()))
TN = (((0,), (0,)), ((), ()))
AHEAD = 4
BEHIND = 2
LOWER_SPLIT, UPPER_SPLIT = 6, 5
CHUNKS = 8
PARTS = 4


def middle_kernel(
    groups,
    size,
    q_in, k_in, v_in, w_in, up_in, mark_in,
    proj_out, dq_out, dk_out, dv_out,
    wbuf, kvbuf, qbuf, up, tags, marks, total, gbuf, obuf, dq_buf, dkv_buf, dk_sum, dv_sum,
    part_out, part_in, proj_buf,
    kv_sem, q_sem, lower_sem, rect_sem, w_sem, chunk_sem,
    in_send, lower_send, rect_send, dq_send, dkv_send, w_send,
    single, out_sem, part_send, part_sem,
):
    rows = q_in.shape[0]
    levels = size // 2
    steps = groups * levels
    blocks = size // 2
    half = blocks * rows
    scaling = HEAD_SIZE ** (-0.5)
    group, ctx = lax.axis_index("fsdp"), lax.axis_index("ctx")
    place, side = ctx // 2, ctx % 2
    owner_place = levels // 2 - 1 + place // (levels // 2)
    across = (group + 2) % groups
    partner = group + 1 - 2 * (group % 2)
    position = ctx % blocks

    def halves(lower):
        split = (LOWER_SPLIT if lower else UPPER_SPLIT) * rows // 8
        return split, pl.ds(0, split), pl.ds(split, rows - split)

    def columns(step, p):
        turn, which = step // groups, step % groups
        late = turn // 2
        source = (1 - late) * (2 - turn) + late * 3 * (3 - turn)
        owner = ((group // 2 + which // 2) % 2) * 2 + (group % 2 + which % 2) % 2
        head = owner * size + 2 * source + p
        return pl.ds(pl.multiple_of(head * HEAD_SIZE, HEAD_SIZE), HEAD_SIZE)

    def remote(source, target, send_sem, receive_sem, device):
        return pltpu.make_async_remote_copy(
            src_ref=source,
            dst_ref=target,
            send_sem=send_sem,
            recv_sem=receive_sem,
            device_id=device,
            device_id_type=pl.DeviceIdType.MESH,
        )

    def arrived(ref, sem):
        remote(ref, ref, sem, sem, {"ctx": (ctx + 1) % size}).wait_recv()

    def sent(ref, sem):
        remote(ref, ref, sem, sem, {"ctx": (ctx + 1) % size}).wait_send()

    def deliver(source, target, send_sem, receive_sem, to):
        @pl.when(to == ctx)
        def _():
            pltpu.make_async_copy(source, target, receive_sem).start()

        @pl.when(to != ctx)
        def _():
            remote(source, target, send_sem, receive_sem, {"ctx": to}).start()

    barrier = pltpu.get_barrier_semaphore()
    greeted = [{"ctx": lax.rem(ctx + step, size)} for step in range(1, size)]
    greeted += [{"fsdp": across}, {"fsdp": partner}]
    for peer in greeted:
        pl.semaphore_signal(barrier, 1, device_id=peer, device_id_type=pl.DeviceIdType.MESH)
    pl.semaphore_wait(barrier, len(greeted))

    own_rows = pl.ds(pl.multiple_of(position * rows, rows), rows)
    key_rows = pl.ds(pl.multiple_of(ctx * rows, rows), rows)

    def piece(chunk):
        size_of = w_in.shape[0] // CHUNKS
        return pl.ds(pl.multiple_of(chunk * size_of, size_of), size_of)

    def send_upstream():
        for p in range(2):
            to = owner_place * 2 + p
            deliver(up_in, up.at[own_rows], single.at[0], single.at[1], to)
            deliver(mark_in, tags.at[position], single.at[2], single.at[3], to)

    def send_step(step):
        for p in range(2):
            to, cols = owner_place * 2 + p, columns(step, p)
            deliver(k_in.at[:, cols], kvbuf.at[step, 0, key_rows], in_send.at[step], kv_sem.at[step], to)
            deliver(v_in.at[:, cols], kvbuf.at[step, 1, key_rows], in_send.at[step], kv_sem.at[step], to)
            deliver(q_in.at[:, cols], qbuf.at[step, own_rows], in_send.at[step], q_sem.at[step], to)

    def leaf(lower):
        split, first_rows, rest = halves(lower)
        turn, opening = (3, 4) if lower else (2, 1)

        def send_piece(chunk):
            remote(
                w_in.at[piece(chunk)], wbuf.at[turn * groups, piece(chunk)],
                w_send.at[0, 0], chunk_sem.at[turn, chunk],
                {"ctx": owner_place * 2 + side},
            ).start()

        if not lower:
            @pl.loop(0, CHUNKS)
            def _(chunk):
                send_piece(chunk)

        @pl.loop(0, steps)
        def _(step):
            @pl.when(step == opening)
            def _():
                send_upstream()

            if lower:
                @pl.when((step >= 1) & (step <= CHUNKS))
                def _():
                    send_piece(step - 1)

            send_step(step)

        arrived(part_in.at[1, rest], part_sem.at[1])
        arrived(part_in.at[2, rest], part_sem.at[2])
        proj_buf[0, rest] = (
            part_in[1, rest].astype(jnp.float32) + part_in[2, rest].astype(jnp.float32)
        ).astype(jnp.bfloat16)
        pltpu.make_async_copy(proj_buf.at[0, rest], proj_out.at[rest], out_sem.at[0]).start()
        sent(w_in, w_send.at[0, 0])
        sent(up.at[pl.ds(0, 2 * rows)], single.at[0])
        sent(tags.at[pl.ds(0, 2)], single.at[2])

        @pl.loop(0, steps)
        def _(step):
            sent(kvbuf.at[step, :, pl.ds(0, 3 * rows)], in_send.at[step])

    def compute(step, base, between=None):
        both = lax.dot_general(up[...], wbuf[step], NT, preferred_element_type=jnp.float32)
        image = marks[...] > 0.5
        gbuf[...] = jnp.where(image, both[:, HEAD_SIZE:], both[:, :HEAD_SIZE]).astype(jnp.bfloat16)
        span = half // 2
        kept = []
        for block in range(2):
            offset = block * span
            finish = base + offset + span
            q = qbuf[step, offset : offset + span, :]
            k = kvbuf[step, 0, :finish, :]
            v = kvbuf[step, 1, :finish, :]
            scores = lax.dot_general(q, k, NT, preferred_element_type=jnp.float32) * scaling
            places = lax.broadcasted_iota(jnp.int32, scores.shape, 0) + (base + offset)
            scores = jnp.where(
                lax.broadcasted_iota(jnp.int32, scores.shape, 1) <= places, scores, -jnp.inf
            )
            raised = jnp.exp(scores - jnp.max(scores, axis=-1, keepdims=True))
            weights = raised * (1.0 / jnp.sum(raised, axis=-1, keepdims=True))
            attention = jnp.dot(
                weights.astype(jnp.bfloat16), v, preferred_element_type=jnp.float32
            ).astype(jnp.bfloat16)
            picked = marks[offset : offset + span, :] > 0.5
            zero = jnp.zeros_like(attention)
            obuf[offset : offset + span, :HEAD_SIZE] = jnp.where(picked, zero, attention)
            obuf[offset : offset + span, HEAD_SIZE:] = jnp.where(picked, attention, zero)
            kept.append((weights, attention))
        width = total.shape[1]
        wide = min(512, width)
        for start in range(0, width, wide):
            total[:, start : start + wide] += jnp.dot(
                obuf[...], wbuf[step, :, start : start + wide], preferred_element_type=jnp.float32
            )
        if between is not None:
            between()
        for block in reversed(range(2)):
            offset = block * span
            finish = base + offset + span
            q = qbuf[step, offset : offset + span, :]
            g = gbuf[offset : offset + span, :]
            k = kvbuf[step, 0, :finish, :]
            v = kvbuf[step, 1, :finish, :]
            weights, attention = kept[block]
            delta = jnp.sum(
                g.astype(jnp.float32) * attention.astype(jnp.float32), axis=-1, keepdims=True
            )
            grad_weights = lax.dot_general(g, v, NT, preferred_element_type=jnp.float32)
            grad_scores = (weights * (grad_weights - delta) * scaling).astype(jnp.bfloat16)
            dq_buf[step, offset : offset + span, :] = jnp.dot(
                grad_scores, k, preferred_element_type=jnp.float32
            ).astype(jnp.bfloat16)
            dk = lax.dot_general(grad_scores, q, TN, preferred_element_type=jnp.float32)
            dv = lax.dot_general(
                weights.astype(jnp.bfloat16), g, TN, preferred_element_type=jnp.float32
            )
            if block == 1:
                dk_sum[:finish, :] = dk
                dv_sum[:finish, :] = dv
            else:
                dk_sum[:finish, :] += dk
                dv_sum[:finish, :] += dv
        dkv_buf[step, 0, : base + half, :] = dk_sum[: base + half, :].astype(jnp.bfloat16)
        dkv_buf[step, 1, : base + half, :] = dv_sum[: base + half, :].astype(jnp.bfloat16)

    def owner(lower):
        base = 0 if lower else half
        first = 0 if lower else blocks
        own_turn = 1 if lower else 0
        middle = {"ctx": (levels - 1 - place) * 2 + side}

        def pass_on(source, turn, part, beyond):
            slot = turn * groups
            remote(
                source, wbuf.at[slot + 2, part], w_send.at[0, turn], w_sem.at[slot + 2],
                {"fsdp": across},
            ).start()
            remote(
                source, wbuf.at[slot + 1, part], w_send.at[1, turn], w_sem.at[slot + 1],
                {"fsdp": partner},
            ).start()
            if beyond is not None:
                remote(
                    source, wbuf.at[slot, part], w_send.at[2, turn], beyond, middle,
                ).start()

        def relay(turn, chunk, beyond):
            part = piece(chunk)
            source = wbuf.at[turn * groups, part]
            arrived(source, chunk_sem.at[turn, chunk])
            pass_on(source, turn, part, chunk_sem.at[turn, chunk] if beyond else None)

        def forward(step):
            arrived(kvbuf.at[step, :, pl.ds(0, half)], kv_sem.at[step])
            remote(
                kvbuf.at[step, :, pl.ds(0, half)], kvbuf.at[step, :, pl.ds(0, half)],
                lower_send.at[step], lower_sem.at[step], middle,
            ).start()

            @pl.when((step >= 1) & (step <= CHUNKS))
            def _():
                relay(3, step - 1, True)

        def spread(buffer, skip, output, step, send_sem, receive_sem):
            cols = columns(step, side)
            for b in range(blocks):
                deliver(
                    buffer.at[pl.ds(skip + b * rows, rows)], output.at[:, cols],
                    send_sem, receive_sem, first + b,
                )

        def spread_keys(step):
            spread(dkv_buf.at[step, 0], base, dk_out, step, dkv_send.at[step], out_sem.at[2])
            spread(dkv_buf.at[step, 1], base, dv_out, step, dkv_send.at[step], out_sem.at[3])

        def finish_keys(step):
            arrived(dkv_buf.at[step, :, pl.ds(half, half)], rect_sem.at[step])
            for t in range(2):
                dkv_buf[step, t, :half, :] = (
                    dkv_buf[step, t, :half, :].astype(jnp.float32)
                    + dkv_buf[step, t, half:, :].astype(jnp.float32)
                ).astype(jnp.bfloat16)
            spread_keys(step)

        own_slot = wbuf.at[own_turn * groups]
        load = pltpu.make_async_copy(w_in, own_slot, w_sem.at[own_turn * groups])
        load.start()

        @pl.loop(0, CHUNKS)
        def _(chunk):
            part = piece(chunk)
            pass_on(w_in.at[part], own_turn, part, chunk_sem.at[own_turn, chunk])

        send_upstream()

        @pl.loop(0, steps)
        def _(step):
            send_step(step)

        total[...] = jnp.zeros_like(total)
        load.wait()

        @pl.loop(0, CHUNKS)
        def _(chunk):
            relay(1 - own_turn, chunk, False)
            if not lower:
                relay(2, chunk, True)

        if lower:
            @pl.loop(0, AHEAD)
            def _(step):
                forward(step)

        arrived(up, single.at[1])
        arrived(tags, single.at[3])
        for b in range(blocks):
            wide = jnp.broadcast_to(tags[b].astype(jnp.float32), (HEAD_SIZE, rows))
            marks[b * rows : (b + 1) * rows, :] = wide.T

        def advance(step, between=None):
            if lower:
                @pl.when(step + AHEAD < steps)
                def _():
                    forward(step + AHEAD)

                @pl.when(step == 1)
                def _():
                    @pl.loop(0, CHUNKS)
                    def _(chunk):
                        relay(2, chunk, False)

            turn, which = step // groups, step % groups

            @pl.when(which == 2)
            def _():
                arrived(wbuf.at[step], w_sem.at[step])
                remote(
                    wbuf.at[step], wbuf.at[step + 1], w_send.at[3, turn], w_sem.at[step + 1],
                    {"fsdp": partner},
                ).start()

            @pl.when(which % 2 == 1)
            def _():
                arrived(wbuf.at[step], w_sem.at[step])

            arrived(qbuf.at[step], q_sem.at[step])
            if not lower:
                arrived(kvbuf.at[step, :, pl.ds(half, half)], kv_sem.at[step])
                arrived(kvbuf.at[step, :, pl.ds(0, half)], lower_sem.at[step])

                @pl.when((step >= 2) & (step < 2 + CHUNKS))
                def _():
                    relay(3, step - 2, False)

            compute(step, base, between)
            spread(dq_buf.at[step], 0, dq_out, step, dq_send.at[step], out_sem.at[1])
            if lower:
                @pl.when(step >= BEHIND)
                def _():
                    finish_keys(step - BEHIND)

            else:
                remote(
                    dkv_buf.at[step, :, pl.ds(0, half)], dkv_buf.at[step, :, pl.ds(half, half)],
                    rect_send.at[step], rect_sem.at[step], middle,
                ).start()
                spread_keys(step)

        split, first_rows, rest = halves(lower)
        leaf_row = 0 if lower else 1
        near_row = 1 - leaf_row
        end_place = 0 if lower else levels - 1
        other = {"ctx": place * 2 + 1 - side}

        def exchange_parts():
            for s in range(2):
                @pl.when(side != s)
                def _():
                    start = (2 * leaf_row + s) * rows
                    part_out[0] = total[start : start + rows, :].astype(jnp.bfloat16)

                @pl.when(side == s)
                def _():
                    start = (2 * leaf_row + s) * rows + split
                    part_out[2, rest] = total[start : start + rows - split, :].astype(
                        jnp.bfloat16
                    )

            remote(
                part_out.at[0, rest], part_in.at[1, rest], part_send.at[1], part_sem.at[1],
                {"ctx": end_place * 2 + 1 - side},
            ).start()
            remote(
                part_out.at[0, first_rows], part_in.at[0, first_rows], part_send.at[0],
                part_sem.at[0], other,
            ).start()
            remote(
                part_out.at[2, rest], part_in.at[2, rest], part_send.at[2], part_sem.at[2],
                {"ctx": end_place * 2 + side},
            ).start()
            for s in range(2):
                @pl.when(side != s)
                def _():
                    start = (2 * near_row + s) * rows
                    part_out[1] = total[start : start + rows, :].astype(jnp.bfloat16)

            remote(
                part_out.at[1], part_in.at[1], part_send.at[3], part_sem.at[3], other
            ).start()

        @pl.loop(0, steps - 1)
        def _(step):
            advance(step)

        advance(steps - 1, exchange_parts)
        if lower:
            @pl.loop(steps - BEHIND, steps - 2)
            def _(step):
                finish_keys(step)

        arrived(part_in.at[0, first_rows], part_sem.at[0])
        for s in range(2):
            @pl.when(side == s)
            def _():
                start = (2 * leaf_row + s) * rows
                proj_buf[0, first_rows] = (
                    total[start : start + split, :] + part_in[0, first_rows].astype(jnp.float32)
                ).astype(jnp.bfloat16)

        remote(
            proj_buf.at[0, first_rows], proj_out.at[first_rows], single.at[4], out_sem.at[0],
            {"ctx": end_place * 2 + side},
        ).start()
        if lower:
            @pl.loop(steps - 2, steps)
            def _(step):
                finish_keys(step)

        arrived(part_in.at[1], part_sem.at[3])
        for s in range(2):
            @pl.when(side == s)
            def _():
                start = (2 * near_row + s) * rows
                proj_buf[1] = (
                    total[start : start + rows, :] + part_in[1].astype(jnp.float32)
                ).astype(jnp.bfloat16)

        pltpu.make_async_copy(proj_buf.at[1], proj_out, out_sem.at[0]).start()
        sent(part_out.at[0, first_rows], part_send.at[0])
        sent(part_out.at[0, rest], part_send.at[1])
        sent(part_out.at[0, rest], part_send.at[2])
        sent(part_out.at[1], part_send.at[3])
        sent(proj_buf.at[0, first_rows], single.at[4])
        sent(up.at[pl.ds(0, rows)], single.at[0])
        sent(tags.at[pl.ds(0, 1)], single.at[2])

        @pl.loop(0, levels)
        def _(turn):
            for kind in (0, 1, 3):
                sent(w_in, w_send.at[kind, turn])

        for turn in (1, 3) if lower else (0, 2):
            sent(w_in, w_send.at[2, turn])

        @pl.loop(0, steps)
        def _(step):
            sent(qbuf.at[step, pl.ds(0, 3 * rows)], in_send.at[step])
            sent(qbuf.at[step, pl.ds(0, 3 * rows)], dq_send.at[step])
            sent(kvbuf.at[step, :, pl.ds(0, 3 * rows)], dkv_send.at[step])
            if lower:
                sent(kvbuf.at[step, :, pl.ds(0, half)], lower_send.at[step])
            else:
                sent(kvbuf.at[step, :, pl.ds(0, half)], rect_send.at[step])

    @pl.when(place == 0)
    def _():
        leaf(True)

    @pl.when(place == levels - 1)
    def _():
        leaf(False)

    @pl.when(place == levels // 2 - 1)
    def _():
        owner(True)

    @pl.when(place == levels // 2)
    def _():
        owner(False)

    for i, output in enumerate((proj_out, dq_out, dk_out, dv_out)):
        arrived(output, out_sem.at[i])


def settle_kernel(*refs):
    sources, targets, held, loads, stores = refs[:4], refs[4:8], refs[8:12], refs[12], refs[13]
    pieces = [(i, h) for i in range(4) for h in range(PARTS)]

    def part(ref, h):
        count = ref.shape[0] // PARTS
        return ref.at[pl.ds(h * count, count)]

    def load(i, h):
        return pltpu.make_async_copy(part(sources[i], h), part(held[i], h), loads.at[i, h])

    def store(i, h):
        return pltpu.make_async_copy(part(held[i], h), part(targets[i], h), stores.at[i, h])

    for i, h in pieces:
        load(i, h).start()
    for i, h in pieces:
        load(i, h).wait()
        store(i, h).start()
    for i, h in pieces:
        store(i, h).wait()


def settle(arrays):
    return pl.pallas_call(
        settle_kernel,
        in_specs=[pl.BlockSpec(memory_space=pl.ANY)] * 4,
        out_specs=[pl.BlockSpec(memory_space=pl.ANY)] * 4,
        out_shape=[jax.ShapeDtypeStruct(a.shape, a.dtype) for a in arrays],
        scratch_shapes=[pltpu.VMEM(a.shape, a.dtype) for a in arrays]
        + [pltpu.SemaphoreType.DMA((4, PARTS))] * 2,
        compiler_params=pltpu.CompilerParams(vmem_limit_bytes=67043328),
    )(*arrays)


def per_device(query_proj, key_proj, value_proj, modality, out_weight, grad_projected):
    size, groups = lax.axis_size("ctx"), lax.axis_size("fsdp")
    rows, width = query_proj.shape[1:]
    piece, out_width = out_weight.shape[1:]
    steps, half, length = groups * size // 2, rows * size // 2, rows * size
    bf, f32, dma = jnp.bfloat16, jnp.float32, pltpu.SemaphoreType.DMA
    results = pl.pallas_call(
        functools.partial(middle_kernel, groups, size),
        in_specs=[pl.BlockSpec(memory_space=pl.ANY)] * 6,
        out_specs=[pl.BlockSpec(memory_space=pl.ANY)] * 4,
        out_shape=[jax.ShapeDtypeStruct((rows, out_width), bf)]
        + [jax.ShapeDtypeStruct((rows, width), bf)] * 3,
        scratch_shapes=[
            pltpu.VMEM((steps, 2 * piece, out_width), bf),
            pltpu.VMEM((steps, 2, length, HEAD_SIZE), bf),
            pltpu.VMEM((steps, half, HEAD_SIZE), bf),
            pltpu.VMEM((half, out_width), bf),
            pltpu.VMEM((size // 2, 1, rows), jnp.int32),
            pltpu.VMEM((half, HEAD_SIZE), f32),
            pltpu.VMEM((half, out_width), f32),
            pltpu.VMEM((half, HEAD_SIZE), bf),
            pltpu.VMEM((half, 2 * HEAD_SIZE), bf),
            pltpu.VMEM((steps, half, HEAD_SIZE), bf),
            pltpu.VMEM((steps, 2, length, HEAD_SIZE), bf),
            pltpu.VMEM((length, HEAD_SIZE), f32),
            pltpu.VMEM((length, HEAD_SIZE), f32),
            pltpu.VMEM((3, rows, out_width), bf),
            pltpu.VMEM((3, rows, out_width), bf),
            pltpu.VMEM((2, rows, out_width), bf),
        ]
        + [dma((steps,))] * 5
        + [dma((size // 2, CHUNKS))]
        + [dma((steps,))] * 5
        + [dma((4, size // 2)), dma((5,)), dma((4,)), dma((4,)), dma((4,))],
        compiler_params=pltpu.CompilerParams(
            collective_id=0, has_side_effects=True, vmem_limit_bytes=67043328
        ),
    )(
        query_proj[0],
        key_proj[0],
        value_proj[0],
        out_weight.reshape(2 * piece, out_width),
        grad_projected[0],
        modality,
    )
    return tuple(a[None] for a in settle(results))


def aligned(mesh, query_shape, weight_shape):
    groups, size = mesh.shape["fsdp"], mesh.shape["ctx"]
    return (
        groups == 4
        and size == 8
        and weight_shape[1] == groups * size * HEAD_SIZE
        and query_shape[0] == groups
        and query_shape[1] <= 1024
    )


def solution(mesh):
    placed = (
        P("fsdp", "ctx", None),
        P("fsdp", "ctx", None),
        P("fsdp", "ctx", None),
        P("fsdp", "ctx"),
        P(None, ("fsdp", "ctx"), None),
        P("fsdp", "ctx", None),
    )
    def whole(*arrays):
        local = per_device if aligned(mesh, arrays[0].shape, arrays[4].shape) else per_device_gathered
        return jax.shard_map(
            local,
            mesh=mesh,
            in_specs=placed,
            out_specs=(P("fsdp", "ctx", None),) * 4,
            check_vma=False,
        )(*arrays)

    return whole
```

```python
import functools

import jax
import jax.numpy as jnp
from jax import lax
from jax.experimental import pallas as pl
from jax.experimental.pallas import tpu as pltpu
from jax.sharding import PartitionSpec as P

HEAD_SIZE = 128


def block_count(length):
    return max(1, min(8, length // 512))


def probabilities(query_block, key_prefix, offset):
    scaling = query_block.shape[-1] ** (-0.5)
    scores = (
        jnp.einsum("hqd,hkd->hqk", query_block, key_prefix, preferred_element_type=jnp.float32)
        * scaling
    )
    query_places = offset + jnp.arange(query_block.shape[1])
    key_places = jnp.arange(key_prefix.shape[1])
    scores = jnp.where(key_places[None, None, :] <= query_places[None, :, None], scores, -jnp.inf)
    highest = jnp.max(scores, axis=-1, keepdims=True)
    raised = jnp.exp(scores - highest)
    return raised / jnp.sum(raised, axis=-1, keepdims=True)


def attend_forward(queries, keys_all, values_all):
    length = queries.shape[1]
    block_rows = length // block_count(length)
    pieces = []
    for block_index in range(length // block_rows):
        offset = block_index * block_rows
        finish = offset + block_rows
        weights = probabilities(queries[:, offset:finish], keys_all[:, :finish], offset).astype(
            jnp.bfloat16
        )
        output = jnp.einsum(
            "hqk,hkd->hqd", weights, values_all[:, :finish], preferred_element_type=jnp.float32
        )
        pieces.append(output.astype(jnp.bfloat16))
    return jnp.concatenate(pieces, axis=1)


def attend_backward(queries, keys_all, values_all, attention, grad_attention):
    length = queries.shape[1]
    block_rows = length // block_count(length)
    scaling = queries.shape[-1] ** (-0.5)
    grad_keys = jnp.zeros(queries.shape, jnp.float32)
    grad_values = jnp.zeros(queries.shape, jnp.float32)
    query_pieces = []
    for block_index in range(length // block_rows):
        offset = block_index * block_rows
        finish = offset + block_rows
        query_block = queries[:, offset:finish]
        weights = probabilities(query_block, keys_all[:, :finish], offset)
        grad_block = grad_attention[:, offset:finish]
        attn_block = attention[:, offset:finish]
        grad_values = grad_values.at[:, :finish].add(
            jnp.einsum(
                "hqk,hqd->hkd",
                weights.astype(jnp.bfloat16),
                grad_block,
                preferred_element_type=jnp.float32,
            )
        )
        grad_weights = jnp.einsum(
            "hqd,hkd->hqk", grad_block, values_all[:, :finish], preferred_element_type=jnp.float32
        )
        row_delta = jnp.sum(
            grad_block.astype(jnp.float32) * attn_block.astype(jnp.float32), axis=-1, keepdims=True
        )
        grad_scores = (weights * (grad_weights - row_delta) * scaling).astype(jnp.bfloat16)
        query_pieces.append(
            jnp.einsum(
                "hqk,hkd->hqd",
                grad_scores,
                keys_all[:, :finish],
                preferred_element_type=jnp.float32,
            ).astype(jnp.bfloat16)
        )
        grad_keys = grad_keys.at[:, :finish].add(
            jnp.einsum("hqk,hqd->hkd", grad_scores, query_block, preferred_element_type=jnp.float32)
        )
    return (
        jnp.concatenate(query_pieces, axis=1),
        grad_keys.astype(jnp.bfloat16),
        grad_values.astype(jnp.bfloat16),
    )


def transposed_product(left, right):
    return lax.dot_general(
        left, right, (((1,), (1,)), ((), ())), preferred_element_type=jnp.float32
    )


def heads_first(flat, length, local_heads):
    return flat.reshape(length, local_heads, HEAD_SIZE).transpose(1, 0, 2)


def heads_last(stacked, length, local_width):
    return stacked.transpose(1, 0, 2).reshape(1, length, local_width)


def per_device_gathered(query_proj, key_proj, value_proj, modality, out_weight, grad_projected):
    context_size = lax.axis_size("ctx")
    row_count = query_proj.shape[1]
    inner_width = query_proj.shape[2]
    length = row_count * context_size
    local_width = inner_width // context_size
    local_heads = local_width // HEAD_SIZE
    head_query, head_key, head_value = (
        lax.all_to_all(query_proj, "ctx", split_axis=2, concat_axis=1, tiled=True),
        lax.all_to_all(key_proj, "ctx", split_axis=2, concat_axis=1, tiled=True),
        lax.all_to_all(value_proj, "ctx", split_axis=2, concat_axis=1, tiled=True),
    )
    head_query = heads_first(head_query, length, local_heads)
    head_key = heads_first(head_key, length, local_heads)
    head_value = heads_first(head_value, length, local_heads)
    attention = attend_forward(head_query, head_key, head_value)
    sending = heads_last(attention, length, local_width)
    attn_rows = lax.all_to_all(sending, "ctx", split_axis=1, concat_axis=2, tiled=True)[0]
    upstream = grad_projected[0]
    weight_piece = lax.all_gather(out_weight, ("fsdp", "ctx"), axis=1, tiled=True)
    text_out = jnp.dot(attn_rows, weight_piece[0], preferred_element_type=jnp.float32)
    image_out = jnp.dot(attn_rows, weight_piece[1], preferred_element_type=jnp.float32)
    text_grad = transposed_product(upstream, weight_piece[0])
    image_grad = transposed_product(upstream, weight_piece[1])
    text_out, image_out, text_grad, image_grad = (text_out, image_out, text_grad, image_grad)
    image_rows = (modality[0] == 1)[:, None]
    projected = jnp.where(image_rows, image_out, text_out).astype(jnp.bfloat16)[None]
    grad_rows = jnp.where(image_rows, image_grad, text_grad).astype(jnp.bfloat16)
    grad_heads = lax.all_to_all(grad_rows[None], "ctx", split_axis=2, concat_axis=1, tiled=True)
    grad_heads = heads_first(grad_heads, length, local_heads)
    grad_q, grad_k, grad_v = attend_backward(
        head_query, head_key, head_value, attention, grad_heads
    )
    grad_query, grad_key, grad_value = (
        lax.all_to_all(
            heads_last(grad_q, length, local_width), "ctx", split_axis=1, concat_axis=2, tiled=True
        ),
        lax.all_to_all(
            heads_last(grad_k, length, local_width), "ctx", split_axis=1, concat_axis=2, tiled=True
        ),
        lax.all_to_all(
            heads_last(grad_v, length, local_width), "ctx", split_axis=1, concat_axis=2, tiled=True
        ),
    )
    return (projected, grad_query, grad_key, grad_value)


NT = (((1,), (1,)), ((), ()))
TN = (((0,), (0,)), ((), ()))
AHEAD = 4
BEHIND = 2
LOWER_SPLIT, UPPER_SPLIT = 6, 5
CHUNKS = 8
PARTS = 4


def middle_kernel(
    groups,
    size,
    q_in, k_in, v_in, w_in, up_in, mark_in,
    proj_out, dq_out, dk_out, dv_out,
    wbuf, kvbuf, qbuf, up, tags, marks, total, gbuf, obuf, dq_buf, dkv_buf, dk_sum, dv_sum,
    part_out, part_in, proj_buf,
    kv_sem, q_sem, lower_sem, rect_sem, w_sem, chunk_sem,
    in_send, lower_send, rect_send, dq_send, dkv_send, w_send,
    single, out_sem, part_send, part_sem,
):
    rows = q_in.shape[0]
    levels = size // 2
    steps = groups * levels
    blocks = size // 2
    half = blocks * rows
    scaling = HEAD_SIZE ** (-0.5)
    group, ctx = lax.axis_index("fsdp"), lax.axis_index("ctx")
    place, side = ctx // 2, ctx % 2
    owner_place = levels // 2 - 1 + place // (levels // 2)
    across = (group + 2) % groups
    partner = group + 1 - 2 * (group % 2)
    position = ctx % blocks

    def halves(lower):
        split = (LOWER_SPLIT if lower else UPPER_SPLIT) * rows // 8
        return split, pl.ds(0, split), pl.ds(split, rows - split)

    def columns(step, p):
        turn, which = step // groups, step % groups
        late = turn // 2
        source = (1 - late) * (2 - turn) + late * 3 * (3 - turn)
        owner = ((group // 2 + which // 2) % 2) * 2 + (group % 2 + which % 2) % 2
        head = owner * size + 2 * source + p
        return pl.ds(pl.multiple_of(head * HEAD_SIZE, HEAD_SIZE), HEAD_SIZE)

    def remote(source, target, send_sem, receive_sem, device):
        return pltpu.make_async_remote_copy(
            src_ref=source,
            dst_ref=target,
            send_sem=send_sem,
            recv_sem=receive_sem,
            device_id=device,
            device_id_type=pl.DeviceIdType.MESH,
        )

    def arrived(ref, sem):
        remote(ref, ref, sem, sem, {"ctx": (ctx + 1) % size}).wait_recv()

    def sent(ref, sem):
        remote(ref, ref, sem, sem, {"ctx": (ctx + 1) % size}).wait_send()

    def deliver(source, target, send_sem, receive_sem, to):
        @pl.when(to == ctx)
        def _():
            pltpu.make_async_copy(source, target, receive_sem).start()

        @pl.when(to != ctx)
        def _():
            remote(source, target, send_sem, receive_sem, {"ctx": to}).start()

    barrier = pltpu.get_barrier_semaphore()
    greeted = [{"ctx": lax.rem(ctx + step, size)} for step in range(1, size)]
    greeted += [{"fsdp": across}, {"fsdp": partner}]
    for peer in greeted:
        pl.semaphore_signal(barrier, 1, device_id=peer, device_id_type=pl.DeviceIdType.MESH)
    pl.semaphore_wait(barrier, len(greeted))

    own_rows = pl.ds(pl.multiple_of(position * rows, rows), rows)
    key_rows = pl.ds(pl.multiple_of(ctx * rows, rows), rows)

    def piece(chunk):
        size_of = w_in.shape[0] // CHUNKS
        return pl.ds(pl.multiple_of(chunk * size_of, size_of), size_of)

    def send_upstream():
        for p in range(2):
            to = owner_place * 2 + p
            deliver(up_in, up.at[own_rows], single.at[0], single.at[1], to)
            deliver(mark_in, tags.at[position], single.at[2], single.at[3], to)

    def send_step(step):
        for p in range(2):
            to, cols = owner_place * 2 + p, columns(step, p)
            deliver(k_in.at[:, cols], kvbuf.at[step, 0, key_rows], in_send.at[step], kv_sem.at[step], to)
            deliver(v_in.at[:, cols], kvbuf.at[step, 1, key_rows], in_send.at[step], kv_sem.at[step], to)
            deliver(q_in.at[:, cols], qbuf.at[step, own_rows], in_send.at[step], q_sem.at[step], to)

    def leaf(lower):
        split, first_rows, rest = halves(lower)
        turn, opening = (3, 4) if lower else (2, 1)

        def send_piece(chunk):
            remote(
                w_in.at[piece(chunk)], wbuf.at[turn * groups, piece(chunk)],
                w_send.at[0, 0], chunk_sem.at[turn, chunk],
                {"ctx": owner_place * 2 + side},
            ).start()

        if not lower:
            @pl.loop(0, CHUNKS)
            def _(chunk):
                send_piece(chunk)

        @pl.loop(0, steps)
        def _(step):
            @pl.when(step == opening)
            def _():
                send_upstream()

            if lower:
                @pl.when((step >= 1) & (step <= CHUNKS))
                def _():
                    send_piece(step - 1)

            send_step(step)

        arrived(part_in.at[1, rest], part_sem.at[1])
        arrived(part_in.at[2, rest], part_sem.at[2])
        proj_buf[0, rest] = (
            part_in[1, rest].astype(jnp.float32) + part_in[2, rest].astype(jnp.float32)
        ).astype(jnp.bfloat16)
        pltpu.make_async_copy(proj_buf.at[0, rest], proj_out.at[rest], out_sem.at[0]).start()
        sent(w_in, w_send.at[0, 0])
        sent(up.at[pl.ds(0, 2 * rows)], single.at[0])
        sent(tags.at[pl.ds(0, 2)], single.at[2])

        @pl.loop(0, steps)
        def _(step):
            sent(kvbuf.at[step, :, pl.ds(0, 3 * rows)], in_send.at[step])

    def compute(step, base, between=None):
        span = half // 2
        kept = []
        for block in range(2):
            offset = block * span
            finish = base + offset + span
            q = qbuf[step, offset : offset + span, :]
            k = kvbuf[step, 0, :finish, :]
            v = kvbuf[step, 1, :finish, :]
            scores = lax.dot_general(q, k, NT, preferred_element_type=jnp.float32) * scaling
            places = lax.broadcasted_iota(jnp.int32, scores.shape, 0) + (base + offset)
            scores = jnp.where(
                lax.broadcasted_iota(jnp.int32, scores.shape, 1) <= places, scores, -jnp.inf
            )
            raised = jnp.exp(scores - jnp.max(scores, axis=-1, keepdims=True))
            weights = raised * (1.0 / jnp.sum(raised, axis=-1, keepdims=True))
            attention = jnp.dot(
                weights.astype(jnp.bfloat16), v, preferred_element_type=jnp.float32
            ).astype(jnp.bfloat16)
            picked = marks[offset : offset + span, :] > 0.5
            zero = jnp.zeros_like(attention)
            obuf[offset : offset + span, :HEAD_SIZE] = jnp.where(picked, zero, attention)
            obuf[offset : offset + span, HEAD_SIZE:] = jnp.where(picked, attention, zero)
            kept.append((weights, attention))
        width = total.shape[1]
        wide = min(512, width)
        for start in range(0, width, wide):
            total[:, start : start + wide] += jnp.dot(
                obuf[...], wbuf[step, :, start : start + wide], preferred_element_type=jnp.float32
            )
        if between is not None:
            between()
        both = lax.dot_general(up[...], wbuf[step], NT, preferred_element_type=jnp.float32)
        image = marks[...] > 0.5
        gbuf[...] = jnp.where(image, both[:, HEAD_SIZE:], both[:, :HEAD_SIZE]).astype(jnp.bfloat16)
        for block in reversed(range(2)):
            offset = block * span
            finish = base + offset + span
            q = qbuf[step, offset : offset + span, :]
            g = gbuf[offset : offset + span, :]
            k = kvbuf[step, 0, :finish, :]
            v = kvbuf[step, 1, :finish, :]
            weights, attention = kept[block]
            delta = jnp.sum(
                g.astype(jnp.float32) * attention.astype(jnp.float32), axis=-1, keepdims=True
            )
            grad_weights = lax.dot_general(g, v, NT, preferred_element_type=jnp.float32)
            grad_scores = (weights * (grad_weights - delta) * scaling).astype(jnp.bfloat16)
            dq_buf[step, offset : offset + span, :] = jnp.dot(
                grad_scores, k, preferred_element_type=jnp.float32
            ).astype(jnp.bfloat16)
            dk = lax.dot_general(grad_scores, q, TN, preferred_element_type=jnp.float32)
            dv = lax.dot_general(
                weights.astype(jnp.bfloat16), g, TN, preferred_element_type=jnp.float32
            )
            if block == 1:
                dk_sum[:finish, :] = dk
                dv_sum[:finish, :] = dv
            else:
                dk_sum[:finish, :] += dk
                dv_sum[:finish, :] += dv
        dkv_buf[step, 0, : base + half, :] = dk_sum[: base + half, :].astype(jnp.bfloat16)
        dkv_buf[step, 1, : base + half, :] = dv_sum[: base + half, :].astype(jnp.bfloat16)

    def owner(lower):
        base = 0 if lower else half
        first = 0 if lower else blocks
        own_turn = 1 if lower else 0
        middle = {"ctx": (levels - 1 - place) * 2 + side}

        def pass_on(source, turn, part, beyond):
            slot = turn * groups
            remote(
                source, wbuf.at[slot + 2, part], w_send.at[0, turn], w_sem.at[slot + 2],
                {"fsdp": across},
            ).start()
            remote(
                source, wbuf.at[slot + 1, part], w_send.at[1, turn], w_sem.at[slot + 1],
                {"fsdp": partner},
            ).start()
            if beyond is not None:
                remote(
                    source, wbuf.at[slot, part], w_send.at[2, turn], beyond, middle,
                ).start()

        def relay(turn, chunk, beyond):
            part = piece(chunk)
            source = wbuf.at[turn * groups, part]
            arrived(source, chunk_sem.at[turn, chunk])
            pass_on(source, turn, part, chunk_sem.at[turn, chunk] if beyond else None)

        def forward(step):
            arrived(kvbuf.at[step, :, pl.ds(0, half)], kv_sem.at[step])
            remote(
                kvbuf.at[step, :, pl.ds(0, half)], kvbuf.at[step, :, pl.ds(0, half)],
                lower_send.at[step], lower_sem.at[step], middle,
            ).start()

            @pl.when((step >= 1) & (step <= CHUNKS))
            def _():
                relay(3, step - 1, True)

        def spread(buffer, skip, output, step, send_sem, receive_sem):
            cols = columns(step, side)
            for b in range(blocks):
                deliver(
                    buffer.at[pl.ds(skip + b * rows, rows)], output.at[:, cols],
                    send_sem, receive_sem, first + b,
                )

        def spread_keys(step):
            spread(dkv_buf.at[step, 0], base, dk_out, step, dkv_send.at[step], out_sem.at[2])
            spread(dkv_buf.at[step, 1], base, dv_out, step, dkv_send.at[step], out_sem.at[3])

        def finish_keys(step):
            arrived(dkv_buf.at[step, :, pl.ds(half, half)], rect_sem.at[step])
            for t in range(2):
                dkv_buf[step, t, :half, :] = (
                    dkv_buf[step, t, :half, :].astype(jnp.float32)
                    + dkv_buf[step, t, half:, :].astype(jnp.float32)
                ).astype(jnp.bfloat16)
            spread_keys(step)

        own_slot = wbuf.at[own_turn * groups]
        load = pltpu.make_async_copy(w_in, own_slot, w_sem.at[own_turn * groups])
        load.start()

        @pl.loop(0, CHUNKS)
        def _(chunk):
            part = piece(chunk)
            pass_on(w_in.at[part], own_turn, part, chunk_sem.at[own_turn, chunk])

        send_upstream()

        @pl.loop(0, steps)
        def _(step):
            send_step(step)

        total[...] = jnp.zeros_like(total)
        load.wait()

        @pl.loop(0, CHUNKS)
        def _(chunk):
            relay(1 - own_turn, chunk, False)
            if not lower:
                relay(2, chunk, True)

        if lower:
            @pl.loop(0, AHEAD)
            def _(step):
                forward(step)

        arrived(up, single.at[1])
        arrived(tags, single.at[3])
        for b in range(blocks):
            wide = jnp.broadcast_to(tags[b].astype(jnp.float32), (HEAD_SIZE, rows))
            marks[b * rows : (b + 1) * rows, :] = wide.T

        def advance(step, between=None):
            if lower:
                @pl.when(step + AHEAD < steps)
                def _():
                    forward(step + AHEAD)

                @pl.when(step == 1)
                def _():
                    @pl.loop(0, CHUNKS)
                    def _(chunk):
                        relay(2, chunk, False)

            turn, which = step // groups, step % groups

            @pl.when(which == 2)
            def _():
                arrived(wbuf.at[step], w_sem.at[step])
                remote(
                    wbuf.at[step], wbuf.at[step + 1], w_send.at[3, turn], w_sem.at[step + 1],
                    {"fsdp": partner},
                ).start()

            @pl.when(which % 2 == 1)
            def _():
                arrived(wbuf.at[step], w_sem.at[step])

            arrived(qbuf.at[step], q_sem.at[step])
            if not lower:
                arrived(kvbuf.at[step, :, pl.ds(half, half)], kv_sem.at[step])
                arrived(kvbuf.at[step, :, pl.ds(0, half)], lower_sem.at[step])

                @pl.when((step >= 2) & (step < 2 + CHUNKS))
                def _():
                    relay(3, step - 2, False)

            compute(step, base, between)
            spread(dq_buf.at[step], 0, dq_out, step, dq_send.at[step], out_sem.at[1])
            if lower:
                @pl.when(step >= BEHIND)
                def _():
                    finish_keys(step - BEHIND)

            else:
                remote(
                    dkv_buf.at[step, :, pl.ds(0, half)], dkv_buf.at[step, :, pl.ds(half, half)],
                    rect_send.at[step], rect_sem.at[step], middle,
                ).start()
                spread_keys(step)

        split, first_rows, rest = halves(lower)
        leaf_row = 0 if lower else 1
        near_row = 1 - leaf_row
        end_place = 0 if lower else levels - 1
        other = {"ctx": place * 2 + 1 - side}

        def exchange_parts():
            for s in range(2):
                @pl.when(side != s)
                def _():
                    start = (2 * leaf_row + s) * rows
                    part_out[0] = total[start : start + rows, :].astype(jnp.bfloat16)

                @pl.when(side == s)
                def _():
                    start = (2 * leaf_row + s) * rows + split
                    part_out[2, rest] = total[start : start + rows - split, :].astype(
                        jnp.bfloat16
                    )

            remote(
                part_out.at[0, rest], part_in.at[1, rest], part_send.at[1], part_sem.at[1],
                {"ctx": end_place * 2 + 1 - side},
            ).start()
            remote(
                part_out.at[0, first_rows], part_in.at[0, first_rows], part_send.at[0],
                part_sem.at[0], other,
            ).start()
            remote(
                part_out.at[2, rest], part_in.at[2, rest], part_send.at[2], part_sem.at[2],
                {"ctx": end_place * 2 + side},
            ).start()
            for s in range(2):
                @pl.when(side != s)
                def _():
                    start = (2 * near_row + s) * rows
                    part_out[1] = total[start : start + rows, :].astype(jnp.bfloat16)

            remote(
                part_out.at[1], part_in.at[1], part_send.at[3], part_sem.at[3], other
            ).start()

        @pl.loop(0, steps - 1)
        def _(step):
            advance(step)

        advance(steps - 1, exchange_parts)
        if lower:
            @pl.loop(steps - BEHIND, steps - 2)
            def _(step):
                finish_keys(step)

        arrived(part_in.at[0, first_rows], part_sem.at[0])
        for s in range(2):
            @pl.when(side == s)
            def _():
                start = (2 * leaf_row + s) * rows
                proj_buf[0, first_rows] = (
                    total[start : start + split, :] + part_in[0, first_rows].astype(jnp.float32)
                ).astype(jnp.bfloat16)

        remote(
            proj_buf.at[0, first_rows], proj_out.at[first_rows], single.at[4], out_sem.at[0],
            {"ctx": end_place * 2 + side},
        ).start()
        if lower:
            @pl.loop(steps - 2, steps)
            def _(step):
                finish_keys(step)

        arrived(part_in.at[1], part_sem.at[3])
        for s in range(2):
            @pl.when(side == s)
            def _():
                start = (2 * near_row + s) * rows
                proj_buf[1] = (
                    total[start : start + rows, :] + part_in[1].astype(jnp.float32)
                ).astype(jnp.bfloat16)

        pltpu.make_async_copy(proj_buf.at[1], proj_out, out_sem.at[0]).start()
        sent(part_out.at[0, first_rows], part_send.at[0])
        sent(part_out.at[0, rest], part_send.at[1])
        sent(part_out.at[0, rest], part_send.at[2])
        sent(part_out.at[1], part_send.at[3])
        sent(proj_buf.at[0, first_rows], single.at[4])
        sent(up.at[pl.ds(0, rows)], single.at[0])
        sent(tags.at[pl.ds(0, 1)], single.at[2])

        @pl.loop(0, levels)
        def _(turn):
            for kind in (0, 1, 3):
                sent(w_in, w_send.at[kind, turn])

        for turn in (1, 3) if lower else (0, 2):
            sent(w_in, w_send.at[2, turn])

        @pl.loop(0, steps)
        def _(step):
            sent(qbuf.at[step, pl.ds(0, 3 * rows)], in_send.at[step])
            sent(qbuf.at[step, pl.ds(0, 3 * rows)], dq_send.at[step])
            sent(kvbuf.at[step, :, pl.ds(0, 3 * rows)], dkv_send.at[step])
            if lower:
                sent(kvbuf.at[step, :, pl.ds(0, half)], lower_send.at[step])
            else:
                sent(kvbuf.at[step, :, pl.ds(0, half)], rect_send.at[step])

    @pl.when(place == 0)
    def _():
        leaf(True)

    @pl.when(place == levels - 1)
    def _():
        leaf(False)

    @pl.when(place == levels // 2 - 1)
    def _():
        owner(True)

    @pl.when(place == levels // 2)
    def _():
        owner(False)

    for i, output in enumerate((proj_out, dq_out, dk_out, dv_out)):
        arrived(output, out_sem.at[i])


def settle_kernel(*refs):
    sources, targets, held, loads, stores = refs[:4], refs[4:8], refs[8:12], refs[12], refs[13]
    pieces = [(i, h) for i in range(4) for h in range(PARTS)]

    def part(ref, h):
        count = ref.shape[0] // PARTS
        return ref.at[pl.ds(h * count, count)]

    def load(i, h):
        return pltpu.make_async_copy(part(sources[i], h), part(held[i], h), loads.at[i, h])

    def store(i, h):
        return pltpu.make_async_copy(part(held[i], h), part(targets[i], h), stores.at[i, h])

    for i, h in pieces:
        load(i, h).start()
    for i, h in pieces:
        load(i, h).wait()
        store(i, h).start()
    for i, h in pieces:
        store(i, h).wait()


def settle(arrays):
    return pl.pallas_call(
        settle_kernel,
        in_specs=[pl.BlockSpec(memory_space=pl.ANY)] * 4,
        out_specs=[pl.BlockSpec(memory_space=pl.ANY)] * 4,
        out_shape=[jax.ShapeDtypeStruct(a.shape, a.dtype) for a in arrays],
        scratch_shapes=[pltpu.VMEM(a.shape, a.dtype) for a in arrays]
        + [pltpu.SemaphoreType.DMA((4, PARTS))] * 2,
        compiler_params=pltpu.CompilerParams(vmem_limit_bytes=67043328),
    )(*arrays)


def per_device(query_proj, key_proj, value_proj, modality, out_weight, grad_projected):
    size, groups = lax.axis_size("ctx"), lax.axis_size("fsdp")
    rows, width = query_proj.shape[1:]
    piece, out_width = out_weight.shape[1:]
    steps, half, length = groups * size // 2, rows * size // 2, rows * size
    bf, f32, dma = jnp.bfloat16, jnp.float32, pltpu.SemaphoreType.DMA
    results = pl.pallas_call(
        functools.partial(middle_kernel, groups, size),
        in_specs=[pl.BlockSpec(memory_space=pl.ANY)] * 6,
        out_specs=[pl.BlockSpec(memory_space=pl.ANY)] * 4,
        out_shape=[jax.ShapeDtypeStruct((rows, out_width), bf)]
        + [jax.ShapeDtypeStruct((rows, width), bf)] * 3,
        scratch_shapes=[
            pltpu.VMEM((steps, 2 * piece, out_width), bf),
            pltpu.VMEM((steps, 2, length, HEAD_SIZE), bf),
            pltpu.VMEM((steps, half, HEAD_SIZE), bf),
            pltpu.VMEM((half, out_width), bf),
            pltpu.VMEM((size // 2, 1, rows), jnp.int32),
            pltpu.VMEM((half, HEAD_SIZE), f32),
            pltpu.VMEM((half, out_width), f32),
            pltpu.VMEM((half, HEAD_SIZE), bf),
            pltpu.VMEM((half, 2 * HEAD_SIZE), bf),
            pltpu.VMEM((steps, half, HEAD_SIZE), bf),
            pltpu.VMEM((steps, 2, length, HEAD_SIZE), bf),
            pltpu.VMEM((length, HEAD_SIZE), f32),
            pltpu.VMEM((length, HEAD_SIZE), f32),
            pltpu.VMEM((3, rows, out_width), bf),
            pltpu.VMEM((3, rows, out_width), bf),
            pltpu.VMEM((2, rows, out_width), bf),
        ]
        + [dma((steps,))] * 5
        + [dma((size // 2, CHUNKS))]
        + [dma((steps,))] * 5
        + [dma((4, size // 2)), dma((5,)), dma((4,)), dma((4,)), dma((4,))],
        compiler_params=pltpu.CompilerParams(
            collective_id=0, has_side_effects=True, vmem_limit_bytes=67043328
        ),
    )(
        query_proj[0],
        key_proj[0],
        value_proj[0],
        out_weight.reshape(2 * piece, out_width),
        grad_projected[0],
        modality,
    )
    return tuple(a[None] for a in settle(results))


def aligned(mesh, query_shape, weight_shape):
    groups, size = mesh.shape["fsdp"], mesh.shape["ctx"]
    return (
        groups == 4
        and size == 8
        and weight_shape[1] == groups * size * HEAD_SIZE
        and query_shape[0] == groups
        and query_shape[1] <= 1024
    )


def solution(mesh):
    placed = (
        P("fsdp", "ctx", None),
        P("fsdp", "ctx", None),
        P("fsdp", "ctx", None),
        P("fsdp", "ctx"),
        P(None, ("fsdp", "ctx"), None),
        P("fsdp", "ctx", None),
    )
    def whole(*arrays):
        local = per_device if aligned(mesh, arrays[0].shape, arrays[4].shape) else per_device_gathered
        return jax.shard_map(
            local,
            mesh=mesh,
            in_specs=placed,
            out_specs=(P("fsdp", "ctx", None),) * 4,
            check_vma=False,
        )(*arrays)

    return whole
```
